512 devices in a mesh: row: 16 (over z, core), col: 8 (over y_hi, x), depth: 4 (over y_lo).
Axes of the slice: x: 4, y: 8 (y_hi: 2, y_lo: 4; y = y_hi * 4 + y_lo), z: 8, core: 2. Of those that a mesh axis runs over, the one named last changes fastest.
Arguments:
- density: bfloat16 [8192, 8192], P('row', 'col'), as said below
Outputs:
- purified: float32 [8192, 8192], P('row', ('col', 'depth'))
Inputs may be any that keep to these rules, and one draw needn't show every extreme that they name: density is symmetric: density[i, j] == density[j, i] for every i and j, for any seed.
All inputs are finite; a program needn't handle non-finite values.
Results may differ from the reference program's by a relative error of at most 0.002.
Values may be sent and summed in bfloat16 or wider, within the bound.
A program may use at most 64 MiB of HBM per device.

```python
import jax
import jax.numpy as jnp

N = 8192


def draw_density(key, part):
    base_key = jax.random.fold_in(key, 11)
    entries = jax.random.normal(base_key, (N, N), jnp.float32) * 0.0707107
    symmetric = 0.5 * (entries + entries.T)
    return jnp.clip(symmetric, -0.35, 0.35).astype(jnp.bfloat16)


def setup_inputs(seed: int = 0) -> dict:
    splits = jax.random.split(jax.random.key(seed), 2)
    return {
        "density": draw_density(jax.random.fold_in(splits[1], 71), 0),
    }


def reference(density):
    square = jnp.dot(density, density, preferred_element_type=jnp.float32).astype(jnp.bfloat16)
    cube_sum = jnp.dot(square, density, preferred_element_type=jnp.float32)
    return 3.0 * square.astype(jnp.float32) - 2.0 * cube_sum
```

```python
import functools

import jax
import jax.numpy as jnp
from jax import lax
from jax.experimental import pallas as pl
from jax.experimental.pallas import tpu as pltpu
from jax.sharding import PartitionSpec as P

MESH = pl.DeviceIdType.MESH
F32 = jnp.float32
BF16 = jnp.bfloat16

CHUNKS = 4
STREAM = 4
SUB = 2
NT = (((1,), (1,)), ((), ()))


def rem(a, b):
    return lax.rem(a, jnp.int32(b))


def div(a, b):
    return lax.div(a, jnp.int32(b))


class Copies:
    def __init__(self):
        self.sent = []

    def start(self, src, dst, send, recv, device, when=None):
        copy = pltpu.make_async_remote_copy(
            src_ref=src, dst_ref=dst, send_sem=send, recv_sem=recv, device_id=device, device_id_type=MESH
        )
        if when is None:
            copy.start()
        else:
            pl.when(when)(copy.start)
        self.sent.append((when, copy.wait_send))

    def finish(self):
        for when, wait in self.sent:
            if when is None:
                wait()
            else:
                pl.when(when)(wait)


def kernel(
    a_ref, out_ref, other, bt, sb, part, relay, raw, summed,
    y_send, y_recv, z_inject, z_forward, z_recv, cross_send, cross_recv, own_send, own_recv, own_local,
    rs_send, rs_recv, ag_send, ag_recv,
):
    rows = a_ref.shape[0]
    width = a_ref.shape[1]
    share = width // 4
    row, col, yl = lax.axis_index("row"), lax.axis_index("col"), lax.axis_index("depth")
    z, core = div(row, 2), rem(row, 2)
    yh, x = div(col, 4), rem(col, 4)
    y = yh * 4 + yl

    def at_z(step, to_core):
        return (rem(z + 8 + step, 8) * 2 + to_core, col, yl)

    def at_y(step):
        to = rem(y + 8 + step, 8)
        return (row, div(to, 4) * 4 + x, rem(to, 4))

    def at_x(step):
        return (row, yh * 4 + rem(x + 4 + step, 4), yl)

    sibling = (z * 2 + 1 - core, col, yl)

    barrier = pltpu.get_barrier_semaphore()
    peers = [at_z(1, 0), at_z(1, 1), at_z(-1, 0), at_z(-1, 1), at_y(1), at_y(-1), at_x(1), at_x(-1), sibling]
    for peer in peers:
        pl.semaphore_signal(barrier, inc=1, device_id=peer, device_id_type=MESH)
    pl.semaphore_wait(barrier, len(peers))

    copies = Copies()

    def wait_recv(dst, sem):
        pltpu.make_async_remote_copy(
            src_ref=dst, dst_ref=dst, send_sem=sem, recv_sem=sem, device_id=sibling, device_id_type=MESH
        ).wait_recv()

    half = rows // 2
    q = rem(z + 8 - 4 * yh, 8)
    source_chip = q < 4
    non_source = q >= 4
    is_source = jnp.logical_and(source_chip, core == div(yl, 2))
    is_sibling = jnp.logical_and(source_chip, core != div(yl, 2))
    parity = rem(yl, 2)
    own_piece = rem(q, 4)
    qq = q + core * (rem(11 - q, 8) - q)
    late = div(rem(qq + 7, 8), 4)
    after_own = 1 - div(qq, 4)
    quarter = half // 2
    sub = quarter // SUB

    def ring_piece(t, of_core, place, is_late):
        piece = (1 - is_late) * rem(place + 7 - t, 4) + is_late * (3 - t)
        return piece + of_core * (3 - 2 * piece)

    def stream_rows(d, j):
        return pl.ds(d * half + (j % 2) * quarter + (j // 2) * (half // STREAM), half // STREAM)

    def inject(h, j):
        d, k = j % 2, j // 2
        offset = d * quarter + k * sub
        src_rows = pl.ds(pl.multiple_of(parity * half + offset, sub), sub)
        src = (a_ref if h == 0 else other).at[src_rows, :]
        dst = bt.at[own_piece, pl.ds(offset, sub), pl.ds(h * width, width)]
        n = h * 4 + j
        to = at_z(1, 0) if d == 0 else at_z(-1, 1)
        copies.start(src, dst, z_inject.at[n], z_recv.at[h * 8 + k], to, is_source)
        copies.start(src, dst, own_send.at[n], own_recv.at[n], sibling, is_source)
        pl.when(is_source)(pltpu.make_async_copy(src, dst, own_local.at[n]).start)

    def stream(d, j):
        at = stream_rows(d, j)
        n = d * STREAM + j
        wait_recv(other.at[at, :], y_recv.at[n])
        last = 3 if d == 0 else 0
        copies.start(
            other.at[at, :], other.at[at, :], y_send.at[8 + n], y_recv.at[n], at_y(1 if d == 0 else -1), yl != last
        )

    def ring(h, t, k):
        n = h * 8 + t * SUB + k
        piece = ring_piece(t, core, qq, late)
        at = bt.at[
            piece, pl.ds(pl.multiple_of(core * quarter + k * sub, sub), sub), pl.ds(h * width, width)
        ]
        if t == 3:
            pl.when(non_source)(lambda: wait_recv(at, z_recv.at[n]))
        else:
            wait_recv(at, z_recv.at[n])
        copies.start(at, at, cross_send.at[n], cross_recv.at[n], sibling, non_source if t == 3 else None)
        forward = {2: qq >= 3, 3: jnp.logical_and(qq >= 4, qq <= 6)}.get(t)
        to = (rem(z + 8 + 1 - 2 * core, 8) * 2 + core, col, yl)
        slot = h * 8 + (t + after_own) * SUB + k
        copies.start(at, at, z_forward.at[n], z_recv.at[slot], to, forward)

    for j in range(STREAM):
        inject(0, j)
        for d in range(2):
            at = stream_rows(d, j)
            first = 3 if d == 0 else 0
            n = d * STREAM + j
            copies.start(
                a_ref.at[at, :], other.at[at, :], y_send.at[n], y_recv.at[n], at_y(1 if d == 0 else -1), yl == first
            )
    for j in range(STREAM):
        for m in (2 * j, 2 * j + 1):
            ring(0, m // SUB, m % SUB)
        stream(0, j)
        stream(1, j)
        inject(1, j)
    for m in range(4 * SUB):
        ring(1, m // SUB, m % SUB)
    sib = 1 - core
    sib_qq = q + sib * (rem(11 - q, 8) - q)
    sib_late = div(rem(sib_qq + 7, 8), 4)
    for h in range(2):
        for t in range(4):
            for k in range(SUB):
                n = h * 8 + t * SUB + k
                piece = ring_piece(t, sib, sib_qq, sib_late)
                at = bt.at[
                    piece, pl.ds(pl.multiple_of(sib * quarter + k * sub, sub), sub), pl.ds(h * width, width)
                ]
                if t == 3:
                    pl.when(non_source)(functools.partial(wait_recv, at, cross_recv.at[n]))
                else:
                    wait_recv(at, cross_recv.at[n])
        for j in range(4):
            offset = (j % 2) * quarter + (j // 2) * sub
            at = bt.at[own_piece, pl.ds(offset, sub), pl.ds(h * width, width)]
            n = h * 4 + j
            pl.when(is_sibling)(functools.partial(wait_recv, at, own_recv.at[n]))
            pl.when(is_source)(
                pltpu.make_async_copy(
                    (a_ref if h == 0 else other).at[
                        pl.ds(pl.multiple_of(parity * half + offset, sub), sub), :
                    ],
                    at,
                    own_local.at[n],
                ).wait
            )

    chunk = rows // CHUNKS
    mid = chunk // 2
    ahead, behind, across = rem(x + 1, 4), rem(x + 3, 4), rem(x + 2, 4)

    def chunk_rows(i, which=None):
        if which is None:
            return pl.ds(i * chunk, chunk)
        return pl.ds(i * chunk + which * mid, mid)

    def multiply(r, i):
        at = chunk_rows(i)
        if r == 0:
            left = jnp.concatenate([a_ref[at, :], other[at, :]], axis=1)
        else:
            left = jnp.concatenate([sb[s, at, :] for s in range(8)], axis=1)

        @pl.loop(0, 4)
        def _(p):
            part[r, p, at, :] = lax.dot_general(left, bt[p], NT, preferred_element_type=F32)

    def rs(r, kind, d, i):
        n = ((r * 3 + kind) * 2 + d) * CHUNKS + i
        return rs_send.at[n], rs_recv.at[n]

    def spread(r, i):
        for d in range(2):
            to = at_x(1 - 2 * d)
            copies.start(part.at[r, across, chunk_rows(i, d), :], relay.at[r, d, i], *rs(r, 0, d, i), to)
        for d in range(2):
            to = at_x(1 - 2 * d)
            piece = ahead if d == 0 else behind
            copies.start(part.at[r, piece, chunk_rows(i, 1 - d), :], raw.at[r, d, i], *rs(r, 1, d, i), to)

    def pass_on(r, i):
        for d in range(2):
            to = at_x(1 - 2 * d)
            piece = ahead if d == 0 else behind
            at = chunk_rows(i, d)
            wait_recv(relay.at[r, d, i], rs(r, 0, d, i)[1])
            part[r, piece, at, :] = part[r, piece, at, :] + relay[r, d, i]
            copies.start(part.at[r, piece, at, :], summed.at[r, d, i], *rs(r, 2, d, i), to)

    def collect(r, i):
        for d in range(2):
            at = chunk_rows(i, d)
            wait_recv(raw.at[r, 1 - d, i], rs(r, 1, 1 - d, i)[1])
            wait_recv(summed.at[r, d, i], rs(r, 2, d, i)[1])
            total = part[r, x, at, :] + raw[r, 1 - d, i] + summed[r, d, i]
            if r == 0:
                sb[yl, at, :] = total.astype(BF16)
            else:
                out_ref[at, :] = 3.0 * sb[yl, at, :].astype(F32) - 2.0 * total

    def slot_of(y_from, y_at):
        return rem(div(y_from, 4) + div(y_at, 4), 2) * 4 + rem(y_from, 4)

    def gather(i, s):
        for d in range(2):
            sign = 1 - 2 * d
            y_from = rem(y + 8 - sign * s, 8)
            at = chunk_rows(i, d if s == 4 else None)
            here = sb.at[slot_of(y_from, y), at, :]
            if s > 0:
                wait_recv(here, ag_recv.at[(d * 5 + s) * CHUNKS + i])
            if s < 4:
                at = chunk_rows(i, d if s == 3 else None)
                y_to = rem(y + 8 + sign, 8)
                copies.start(
                    sb.at[slot_of(y_from, y), at, :],
                    sb.at[slot_of(y_from, y_to), at, :],
                    ag_send.at[(d * 5 + s) * CHUNKS + i],
                    ag_recv.at[(d * 5 + s + 1) * CHUNKS + i],
                    at_y(sign),
                )

    period = 4.8
    events = []
    for i in range(CHUNKS):
        t = i * period
        events += [
            (t, lambda i=i: (multiply(0, i), spread(0, i))),
            (t + 2.7, lambda i=i: pass_on(0, i)),
            (t + 6.6, lambda i=i: (collect(0, i), gather(i, 0))),
            (t + 9.1, lambda i=i: gather(i, 1)),
            (t + 11.6, lambda i=i: gather(i, 2)),
            (t + 14.1, lambda i=i: gather(i, 3)),
            (t + 16.1, lambda i=i: (gather(i, 4), multiply(1, i), spread(1, i))),
            (t + 18.8, lambda i=i: pass_on(1, i)),
            (t + 22.7, lambda i=i: collect(1, i)),
        ]
    for _, event in sorted(events, key=lambda e: e[0]):
        event()
    copies.finish()


def on_device(density):
    rows, width = density.shape
    share = width // 4
    chunk = rows // CHUNKS
    dma = pltpu.SemaphoreType.DMA
    return pl.pallas_call(
        kernel,
        out_shape=jax.ShapeDtypeStruct((rows, share), F32),
        in_specs=[pl.BlockSpec(memory_space=pltpu.VMEM)],
        out_specs=pl.BlockSpec(memory_space=pltpu.VMEM),
        scratch_shapes=[
            pltpu.VMEM((rows, width), BF16),
            pltpu.VMEM((4, share, 2 * width), BF16),
            pltpu.VMEM((8, rows, share), BF16),
            pltpu.VMEM((2, 4, rows, share), F32),
            pltpu.VMEM((2, 2, CHUNKS, chunk // 2, share), F32),
            pltpu.VMEM((2, 2, CHUNKS, chunk // 2, share), F32),
            pltpu.VMEM((2, 2, CHUNKS, chunk // 2, share), F32),
            dma((16,)),
            dma((8,)),
            dma((8,)),
            dma((16,)),
            dma((16,)),
            dma((16,)),
            dma((16,)),
            dma((8,)),
            dma((8,)),
            dma((8,)),
            dma((12 * CHUNKS,)),
            dma((12 * CHUNKS,)),
            dma((10 * CHUNKS,)),
            dma((10 * CHUNKS,)),
        ],
        compiler_params=pltpu.CompilerParams(
            collective_id=0, has_side_effects=True, vmem_limit_bytes=48 * 1024 * 1024
        ),
    )(density)


def solution(mesh):
    return jax.shard_map(
        on_device, mesh=mesh, in_specs=(P("row", "col"),), out_specs=P("row", ("col", "depth")), check_vma=False
    )
```

```python
import functools

import jax
import jax.numpy as jnp
from jax import lax
from jax.experimental import pallas as pl
from jax.experimental.pallas import tpu as pltpu
from jax.sharding import PartitionSpec as P

MESH = pl.DeviceIdType.MESH
F32 = jnp.float32
BF16 = jnp.bfloat16

CHUNKS = 4
STREAM = 8
HOP = 2
TICKS = 16 + 4 * HOP


def rem(a, b):
    return lax.rem(a, jnp.int32(b))


def div(a, b):
    return lax.div(a, jnp.int32(b))


def rel_half(z, yh):
    return rem(div(z, 4) + yh, 2)


class Copies:
    def __init__(self):
        self.sent = []

    def start(self, src, dst, send, recv, device, when=None):
        copy = pltpu.make_async_remote_copy(
            src_ref=src, dst_ref=dst, send_sem=send, recv_sem=recv, device_id=device, device_id_type=MESH
        )
        if when is None:
            copy.start()
        else:
            pl.when(when)(copy.start)
        self.sent.append((when, copy.wait_send))

    def finish(self):
        for when, wait in self.sent:
            if when is None:
                wait()
            else:
                pl.when(when)(wait)


def kernel(
    a_ref, out_ref, other, bt, sb, part, relay, raw, summed,
    x_send, x_recv, y_send, y_recv, z_inject, z_forward, z_recv, cross_send, cross_recv, own_send, own_recv, own_local,
    rs_send, rs_recv, ag_send, ag_recv,
):
    rows = a_ref.shape[0]
    width = a_ref.shape[1]
    share = width // 4
    row, col, yl = lax.axis_index("row"), lax.axis_index("col"), lax.axis_index("depth")
    z, core = div(row, 2), rem(row, 2)
    yh, x = div(col, 4), rem(col, 4)
    y = yh * 4 + yl

    def at_z(step, to_core):
        return (rem(z + 8 + step, 8) * 2 + to_core, col, yl)

    def at_y(step):
        to = rem(y + 8 + step, 8)
        return (row, div(to, 4) * 4 + x, rem(to, 4))

    def at_x(step):
        return (row, yh * 4 + rem(x + 4 + step, 4), yl)

    sibling = (z * 2 + 1 - core, col, yl)

    barrier = pltpu.get_barrier_semaphore()
    peers = [at_z(1, 0), at_z(1, 1), at_z(-1, 0), at_z(-1, 1), at_y(1), at_y(-1), at_x(1), at_x(-1), at_x(2), sibling]
    for peer in peers:
        pl.semaphore_signal(barrier, inc=1, device_id=peer, device_id_type=MESH)
    pl.semaphore_wait(barrier, len(peers))

    copies = Copies()

    def remote(src, dst, send, recv, device):
        return pltpu.make_async_remote_copy(
            src_ref=src, dst_ref=dst, send_sem=send, recv_sem=recv, device_id=device, device_id_type=MESH
        )

    def start(src, dst, send, recv, device):
        remote(src, dst, send, recv, device).start()

    def wait_recv(dst, sem):
        remote(dst, dst, sem, sem, sibling).wait_recv()

    def wait_send(src, sem):
        remote(src, src, sem, sem, sibling).wait_send()

    half = rows // 2
    strip = half // STREAM
    block = half
    up = rem(z + 8 - x, 4)
    w = up + core * (rem(4 - up, 4) - up)
    is_source = w == 0
    away = w + 4 * (1 - lax.min(w, jnp.int32(1)))
    passed = rel_half(rem(z + 8 - (1 - 2 * core) * away, 8), yh)
    held = rel_half(z, yh)
    next_z = at_z(1 - 2 * core, core)

    def gray(e):
        return e + div(e, 2) * (5 - 2 * e)

    def tile(which, e, c, k):
        at = pl.ds(pl.multiple_of(c * rows + k * block, block), block)
        return bt.at[which, rem(x + gray(e), 4), at, :]

    own_cols = pl.ds(pl.multiple_of(yl * share, share), share)

    def inject(i, e, k, src):
        dst = tile(held, e, core, k)
        m = i * 2 + core
        start(src, dst, z_inject.at[i], z_recv.at[m], at_z(1, 0))
        start(src, dst, z_inject.at[8 + i], z_recv.at[m], at_z(-1, 1))
        start(src, dst, own_send.at[i], own_recv.at[i], sibling)

    def ring_chunk(m):
        i, c = div(m, 2), rem(m, 2)
        return tile(passed, div(i, 2), c, rem(i, 2)), c

    def passes(c):
        return jnp.logical_or(w < 3, c == core)

    def ring(m):
        at, c = ring_chunk(m)

        @pl.when(jnp.logical_or(w > 0, c == core))
        def _():
            wait_recv(at, z_recv.at[m])
            start(at, at, cross_send.at[m], cross_recv.at[m], sibling)

            @pl.when(jnp.logical_and(w > 0, passes(c)))
            def _():
                start(at, at, z_forward.at[m], z_recv.at[m], next_z)

    def strip_rows(d, j):
        return pl.ds(pl.multiple_of(d * half + j * strip, strip), strip)

    def stream(d, j):
        at = strip_rows(d, j)
        n = d * STREAM + j
        wait_recv(other.at[at, :], y_recv.at[n])

        @pl.when(yl != 3 * (1 - d))
        def _():
            start(other.at[at, :], other.at[at, :], y_send.at[n], y_recv.at[n], at_y(1 - 2 * d))

    for k in range(2):
        src = a_ref.at[pl.ds(k * block, block), own_cols]

        @pl.when(is_source)
        def _():
            inject(k, jnp.int32(0), jnp.int32(k), src)
            pltpu.make_async_copy(src, tile(held, jnp.int32(0), core, jnp.int32(k)), own_local.at[k]).start()

        @pl.when(w > 0)
        def _():
            to = rem(z, 4)
            e = gray(rem(x + 4 - to, 4))
            dst = bt.at[held, x, pl.ds(pl.multiple_of(core * rows + k * block, block), block), :]
            start(src, dst, x_send.at[k], x_recv.at[e * 2 + k], (row, yh * 4 + to, yl))

    for d in range(2):

        @pl.when(yl == 3 * (1 - d))
        def _():
            for j in range(STREAM):
                at = strip_rows(d, j)
                n = d * STREAM + j
                start(a_ref.at[at, :], other.at[at, :], y_send.at[n], y_recv.at[n], at_y(1 - 2 * d))

    @pl.loop(0, TICKS)
    def _(tick):
        i = div(tick, 2) + 1

        @pl.when(is_source & (rem(tick, 2) == 0) & (i >= 2) & (i < 8))
        def _():
            e, k = div(i, 2), rem(i, 2)
            src = tile(held, e, core, k)
            wait_recv(src, x_recv.at[i])
            inject(i, e, k, src)

        m = tick - HOP * away

        @pl.when((m >= 0) & (m < 16))
        def _():
            ring(m)

        for d in range(2):
            j = tick - HOP * (yl + 1 if d == 0 else 4 - yl)

            @pl.when((j >= 0) & (j < STREAM))
            def _():
                stream(d, j)

    sib_w = rem(4 - w, 4)
    sib_away = sib_w + 4 * (1 - lax.min(sib_w, jnp.int32(1)))
    sib_passed = rel_half(rem(z + 8 + (1 - 2 * core) * sib_away, 8), yh)

    @pl.loop(0, 16)
    def _(m):
        i, c = div(m, 2), rem(m, 2)

        @pl.when(jnp.logical_or(w > 0, c != core))
        def _():
            wait_recv(tile(sib_passed, div(i, 2), c, rem(i, 2)), cross_recv.at[m])

    @pl.when(is_source)
    def _():
        for k in range(2):
            src = a_ref.at[pl.ds(k * block, block), own_cols]
            pltpu.make_async_copy(src, tile(held, jnp.int32(0), core, jnp.int32(k)), own_local.at[k]).wait()

        @pl.loop(0, 8)
        def _(i):
            wait_recv(tile(held, div(i, 2), 1 - core, rem(i, 2)), own_recv.at[i])

    def finish_operands():
        for k in range(2):

            @pl.when(w > 0)
            def _():
                wait_send(bt.at[held, x, pl.ds(0, block), :], x_send.at[k])

        @pl.when(is_source)
        def _():
            @pl.loop(0, 8)
            def _(i):
                src = tile(held, div(i, 2), core, rem(i, 2))
                wait_send(src, z_inject.at[i])
                wait_send(src, z_inject.at[8 + i])
                wait_send(src, own_send.at[i])

        @pl.loop(0, 16)
        def _(m):
            at, c = ring_chunk(m)

            @pl.when(jnp.logical_or(w > 0, c == core))
            def _():
                wait_send(at, cross_send.at[m])

                @pl.when(jnp.logical_and(w > 0, passes(c)))
                def _():
                    wait_send(at, z_forward.at[m])

        @pl.loop(0, 2 * STREAM)
        def _(n):
            at = pl.ds(pl.multiple_of(n * strip, strip), strip)
            wait_send(other.at[at, :], y_send.at[n])

    chunk = rows // CHUNKS
    mid = chunk // 2
    ahead, behind, across = rem(x + 1, 4), rem(x + 3, 4), rem(x + 2, 4)

    def chunk_rows(i, which=None):
        if which is None:
            return pl.ds(i * chunk, chunk)
        return pl.ds(i * chunk + which * mid, mid)

    def multiply(r, i):
        at = chunk_rows(i)
        if r == 0:
            left = jnp.concatenate([a_ref[at, :], other[at, :]], axis=1)
        else:
            left = jnp.concatenate([sb[s, at, :] for s in range(8)], axis=1)

        @pl.loop(0, 4)
        def _(p):
            right = jnp.concatenate([bt[0, p], bt[1, p]], axis=0)
            part[r, p, at, :] = jnp.dot(left, right, preferred_element_type=F32)

    def rs(r, kind, d, i):
        n = ((r * 3 + kind) * 2 + d) * CHUNKS + i
        return rs_send.at[n], rs_recv.at[n]

    def spread(r, i):
        for d in range(2):
            to = at_x(1 - 2 * d)
            copies.start(part.at[r, across, chunk_rows(i, d), :], relay.at[r, d, i], *rs(r, 0, d, i), to)
        for d in range(2):
            to = at_x(1 - 2 * d)
            piece = ahead if d == 0 else behind
            copies.start(part.at[r, piece, chunk_rows(i, 1 - d), :], raw.at[r, d, i], *rs(r, 1, d, i), to)

    def pass_on(r, i):
        for d in range(2):
            to = at_x(1 - 2 * d)
            piece = ahead if d == 0 else behind
            at = chunk_rows(i, d)
            wait_recv(relay.at[r, d, i], rs(r, 0, d, i)[1])
            part[r, piece, at, :] = part[r, piece, at, :] + relay[r, d, i]
            copies.start(part.at[r, piece, at, :], summed.at[r, d, i], *rs(r, 2, d, i), to)

    def collect(r, i):
        for d in range(2):
            at = chunk_rows(i, d)
            wait_recv(raw.at[r, 1 - d, i], rs(r, 1, 1 - d, i)[1])
            wait_recv(summed.at[r, d, i], rs(r, 2, d, i)[1])
            total = part[r, x, at, :] + raw[r, 1 - d, i] + summed[r, d, i]
            if r == 0:
                sb[yl, at, :] = total.astype(BF16)
            else:
                out_ref[at, :] = 3.0 * sb[yl, at, :].astype(F32) - 2.0 * total

    def slot_of(y_from, y_at):
        return rem(div(y_from, 4) + div(y_at, 4), 2) * 4 + rem(y_from, 4)

    def gather(i, s):
        for d in range(2):
            sign = 1 - 2 * d
            y_from = rem(y + 8 - sign * s, 8)
            at = chunk_rows(i, d if s == 4 else None)
            here = sb.at[slot_of(y_from, y), at, :]
            if s > 0:
                wait_recv(here, ag_recv.at[(d * 5 + s) * CHUNKS + i])
            if s < 4:
                at = chunk_rows(i, d if s == 3 else None)
                y_to = rem(y + 8 + sign, 8)
                copies.start(
                    sb.at[slot_of(y_from, y), at, :],
                    sb.at[slot_of(y_from, y_to), at, :],
                    ag_send.at[(d * 5 + s) * CHUNKS + i],
                    ag_recv.at[(d * 5 + s + 1) * CHUNKS + i],
                    at_y(sign),
                )

    period = 4.8
    events = []
    for i in range(CHUNKS):
        t = i * period
        events += [
            (t, lambda i=i: (multiply(0, i), spread(0, i))),
            (t + 2.7, lambda i=i: pass_on(0, i)),
            (t + 6.6, lambda i=i: (collect(0, i), gather(i, 0))),
            (t + 9.1, lambda i=i: gather(i, 1)),
            (t + 11.6, lambda i=i: gather(i, 2)),
            (t + 14.1, lambda i=i: gather(i, 3)),
            (t + 16.1, lambda i=i: (gather(i, 4), multiply(1, i), spread(1, i))),
            (t + 18.8, lambda i=i: pass_on(1, i)),
            (t + 22.7, lambda i=i: collect(1, i)),
        ]
    for _, event in sorted(events, key=lambda e: e[0]):
        event()
    copies.finish()
    finish_operands()


def on_device(density):
    rows, width = density.shape
    share = width // 4
    chunk = rows // CHUNKS
    dma = pltpu.SemaphoreType.DMA
    return pl.pallas_call(
        kernel,
        out_shape=jax.ShapeDtypeStruct((rows, share), F32),
        in_specs=[pl.BlockSpec(memory_space=pltpu.VMEM)],
        out_specs=pl.BlockSpec(memory_space=pltpu.VMEM),
        scratch_shapes=[
            pltpu.VMEM((rows, width), BF16),
            pltpu.VMEM((2, 4, 2 * rows, share), BF16),
            pltpu.VMEM((8, rows, share), BF16),
            pltpu.VMEM((2, 4, rows, share), F32),
            pltpu.VMEM((2, 2, CHUNKS, chunk // 2, share), F32),
            pltpu.VMEM((2, 2, CHUNKS, chunk // 2, share), F32),
            pltpu.VMEM((2, 2, CHUNKS, chunk // 2, share), F32),
            dma((2,)),
            dma((8,)),
            dma((2 * STREAM,)),
            dma((2 * STREAM,)),
            dma((16,)),
            dma((16,)),
            dma((16,)),
            dma((16,)),
            dma((16,)),
            dma((8,)),
            dma((8,)),
            dma((2,)),
            dma((12 * CHUNKS,)),
            dma((12 * CHUNKS,)),
            dma((10 * CHUNKS,)),
            dma((10 * CHUNKS,)),
        ],
        compiler_params=pltpu.CompilerParams(
            collective_id=0, has_side_effects=True, vmem_limit_bytes=48 * 1024 * 1024
        ),
    )(density)


def solution(mesh):
    return jax.shard_map(
        on_device, mesh=mesh, in_specs=(P("row", "col"),), out_specs=P("row", ("col", "depth")), check_vma=False
    )
```

```python
import jax
import jax.numpy as jnp
from jax import lax
from jax.experimental import pallas as pl
from jax.experimental.pallas import tpu as pltpu
from jax.sharding import PartitionSpec as P

MESH = pl.DeviceIdType.MESH
F32 = jnp.float32
BF16 = jnp.bfloat16

GROUPS = 2
SQUARE = 4
CUBE = 4
SPLIT = 2
UNITS = 8 * SPLIT
STREAM = 8 * SPLIT
HOP = 5
TICK = 0.75
TICKS = 2 * UNITS + 4 * HOP
PASS, COLLECT, RING, PERIOD = 4.1, 7.8, 3.5, 2.4
PASS_CUBE, COLLECT_CUBE, PERIOD_CUBE = 5.5, 10.5, 4.5


def rem(a, b):
    return lax.rem(a, jnp.int32(b))


def div(a, b):
    return lax.div(a, jnp.int32(b))


def rel_half(z, yh):
    return rem(div(z, 4) + yh, 2)


def gray(e):
    return e + div(e, 2) * (5 - 2 * e)


def kernel(
    a_hbm, out_ref, a_ref, own, other, bt, sb, part1, part2, relay1, raw1, summed1, relay2, raw2, summed2,
    x_send, x_recv, y_send, y_recv, z_inject, z_forward, z_recv, cross_send, cross_recv, own_send, own_recv, own_local, load,
    rs1_send, rs1_recv, rs2_send, rs2_recv, ag_send, ag_recv,
):
    rows, width = a_hbm.shape
    share = width // 4
    cols = share // GROUPS
    row, col, yl = lax.axis_index("row"), lax.axis_index("col"), lax.axis_index("depth")
    z, core = div(row, 2), rem(row, 2)
    yh, x = div(col, 4), rem(col, 4)
    y = yh * 4 + yl

    def at_z(step, to_core):
        return (rem(z + 8 + step, 8) * 2 + to_core, col, yl)

    def at_y(step):
        to = rem(y + 8 + step, 8)
        return (row, div(to, 4) * 4 + x, rem(to, 4))

    def at_x(step):
        return (row, yh * 4 + rem(x + 4 + step, 4), yl)

    sibling = (z * 2 + 1 - core, col, yl)

    loads = [
        pltpu.make_async_copy(
            a_hbm.at[:, pl.ds(pl.multiple_of(yl * share + g * cols, cols), cols)], own.at[g], load.at[g]
        )
        for g in range(GROUPS)
    ] + [pltpu.make_async_copy(a_hbm, a_ref, load.at[GROUPS])]
    for copy in loads:
        copy.start()

    barrier = pltpu.get_barrier_semaphore()
    peers = [at_z(1, 0), at_z(1, 1), at_z(-1, 0), at_z(-1, 1), at_y(1), at_y(-1), at_x(1), at_x(-1), at_x(2), sibling]
    for peer in peers:
        pl.semaphore_signal(barrier, inc=1, device_id=peer, device_id_type=MESH)
    for copy in loads:
        copy.wait()
    pl.semaphore_wait(barrier, len(peers))

    def remote(src, dst, send, recv, device):
        return pltpu.make_async_remote_copy(
            src_ref=src, dst_ref=dst, send_sem=send, recv_sem=recv, device_id=device, device_id_type=MESH
        )

    def start(src, dst, send, recv, device):
        remote(src, dst, send, recv, device).start()

    def wait_recv(dst, sem):
        remote(dst, dst, sem, sem, sibling).wait_recv()

    def wait_send(src, sem):
        remote(src, src, sem, sem, sibling).wait_send()

    half = rows // 2
    strip = half // STREAM
    up = rem(z + 8 - x, 4)
    w = up + core * (rem(4 - up, 4) - up)
    is_source = w == 0
    away = w + 4 * (1 - lax.min(w, jnp.int32(1)))
    passed = rel_half(rem(z + 8 - (1 - 2 * core) * away, 8), yh)
    held = rel_half(z, yh)
    next_z = at_z(1 - 2 * core, core)

    unit = rows // SPLIT

    def tile(which, i, c):
        n, k = div(i, SPLIT), rem(i, SPLIT)
        u = div(n + 1, 3)
        others = lax.min(u, jnp.int32(1))
        g = others * (u - 1) + (1 - others) * n
        e = others * (rem(n + 1, 3) + 1)
        at = pl.ds(pl.multiple_of(c * rows + k * unit, unit), unit)
        return bt.at[which, g, rem(x + gray(e), 4), at, :]

    def own_piece(g, k):
        return own.at[g, pl.ds(k * unit, unit), :]

    def own_copy(g, k):
        i = g * SPLIT + k
        return pltpu.make_async_copy(own_piece(g, k), tile(held, jnp.int32(i), core), own_local.at[i])

    def inject(i, src):
        dst = tile(held, i, core)
        m = i * 2 + core
        start(src, dst, z_inject.at[i], z_recv.at[m], at_z(1, 0))
        start(src, dst, z_inject.at[UNITS + i], z_recv.at[m], at_z(-1, 1))
        start(src, dst, own_send.at[i], own_recv.at[i], sibling)

    def passes(c):
        return (w > 0) & ((w < 3) | (c == core))

    def ring(m):
        i, c = div(m, 2), rem(m, 2)
        at = tile(passed, i, c)

        @pl.when((w > 0) | (c == core))
        def _():
            wait_recv(at, z_recv.at[m])

            @pl.when(passes(c))
            def _():
                start(at, at, z_forward.at[m], z_recv.at[m], next_z)

            start(at, at, cross_send.at[m], cross_recv.at[m], sibling)

    def strip_rows(d, j):
        return pl.ds(pl.multiple_of(d * half + j * strip, strip), strip)

    def stream(d, j):
        at = strip_rows(d, j)
        n = d * STREAM + j
        wait_recv(other.at[at, :], y_recv.at[n])

        @pl.when(yl != 3 * (1 - d))
        def _():
            start(other.at[at, :], other.at[at, :], y_send.at[n], y_recv.at[n], at_y(1 - 2 * d))

    @pl.when(is_source)
    def _():
        for g in range(GROUPS):
            for k in range(SPLIT):
                inject(jnp.int32(g * SPLIT + k), own_piece(g, k))
        for g in range(GROUPS):
            for k in range(SPLIT):
                own_copy(g, k).start()

    @pl.when(w > 0)
    def _():
        to = rem(z, 4)
        e = gray(rem(x + 4 - to, 4))
        for g in range(GROUPS):
            for k in range(SPLIT):
                dst = bt.at[held, g, x, pl.ds(pl.multiple_of(core * rows + k * unit, unit), unit), :]
                arrival = x_recv.at[(e + 1 + 3 * g) * SPLIT + k]
                start(own_piece(g, k), dst, x_send.at[g * SPLIT + k], arrival, (row, yh * 4 + to, yl))

    for d in range(2):

        @pl.when(yl == 3 * (1 - d))
        def _():
            for j in range(STREAM):
                at = strip_rows(d, j)
                n = d * STREAM + j
                start(a_ref.at[at, :], other.at[at, :], y_send.at[n], y_recv.at[n], at_y(1 - 2 * d))

    def tick(t):
        i = t

        @pl.when(is_source & (i >= 2 * SPLIT) & (i < UNITS))
        def _():
            src = tile(held, i, core)
            wait_recv(src, x_recv.at[i])
            inject(i, src)

        m = t - HOP * away

        @pl.when((m >= 0) & (m < 2 * UNITS))
        def _():
            ring(m)

        for d in range(2):
            j = t - HOP * (yl + 1 if d == 0 else 4 - yl)

            @pl.when((j >= 0) & (j < STREAM))
            def _():
                stream(d, j)

    sib_w = rem(4 - w, 4)
    sib_away = sib_w + 4 * (1 - lax.min(sib_w, jnp.int32(1)))
    sib_passed = rel_half(rem(z + 8 + (1 - 2 * core) * sib_away, 8), yh)

    def arrived(g):
        first, after = (0, 5 * SPLIT) if g == 0 else (5 * SPLIT, UNITS)

        @pl.loop(2 * first, 2 * after)
        def _(m):
            i, c = div(m, 2), rem(m, 2)

            @pl.when((w > 0) | (c != core))
            def _():
                wait_recv(tile(sib_passed, i, c), cross_recv.at[m])

        @pl.when(is_source)
        def _():
            if g == 0:
                for i in range(2 * SPLIT):
                    own_copy(i // SPLIT, i % SPLIT).wait()

            @pl.loop(first, after)
            def _(i):
                wait_recv(tile(held, i, 1 - core), own_recv.at[i])

    def finish_operands():
        @pl.when(w > 0)
        def _():
            for i in range(2 * SPLIT):
                wait_send(bt.at[held, 0, x, pl.ds(0, unit), :], x_send.at[i])

        @pl.when(is_source)
        def _():
            @pl.loop(0, UNITS)
            def _(i):
                src = tile(held, i, core)
                wait_send(src, z_inject.at[i])
                wait_send(src, z_inject.at[UNITS + i])
                wait_send(src, own_send.at[i])

        @pl.loop(0, 2 * UNITS)
        def _(m):
            i, c = div(m, 2), rem(m, 2)
            at = tile(passed, i, c)

            @pl.when((w > 0) | (c == core))
            def _():
                wait_send(at, cross_send.at[m])

                @pl.when(passes(c))
                def _():
                    wait_send(at, z_forward.at[m])

        @pl.loop(0, 2 * STREAM)
        def _(n):
            at = pl.ds(pl.multiple_of(n * strip, strip), strip)
            wait_send(other.at[at, :], y_send.at[n])

    ahead, behind, across = rem(x + 1, 4), rem(x + 3, 4), rem(x + 2, 4)
    sent = []

    def send(src, dst, send_sem, recv_sem, device):
        copy = remote(src, dst, send_sem, recv_sem, device)
        copy.start()
        sent.append(copy.wait_send)

    class Sum:
        def __init__(self, part, relay, raw, summed, sends, recvs, chunk):
            self.part, self.relay, self.raw, self.summed = part, relay, raw, summed
            self.sends, self.recvs, self.mid = sends, recvs, chunk // 2
            self.slots = relay.shape[1]

        def at(self, piece, i, which):
            g, r = i
            rows_at = pl.ds((2 * r + which) * self.mid, self.mid)
            return (g, piece, rows_at, slice(None)) if g is not None else (piece, rows_at, slice(None))

        def slot(self, i):
            return i[0] * SQUARE + i[1] if i[0] is not None else i[1]

        def sems(self, kind, d, i):
            n = (kind * 2 + d) * self.slots + self.slot(i)
            return self.sends.at[n], self.recvs.at[n]

        def spread(self, i):
            n = self.slot(i)
            for d in range(2):
                src = self.part.at[self.at(across, i, d)]
                send(src, self.relay.at[d, n], *self.sems(0, d, i), at_x(1 - 2 * d))
            for d in range(2):
                src = self.part.at[self.at(ahead if d == 0 else behind, i, 1 - d)]
                send(src, self.raw.at[d, n], *self.sems(1, d, i), at_x(1 - 2 * d))

        def pass_on(self, i):
            n = self.slot(i)
            for d in range(2):
                wait_recv(self.relay.at[d, n], self.sems(0, d, i)[1])
                at = self.at(ahead if d == 0 else behind, i, d)
                self.part[at] = self.part[at] + self.relay[d, n]
                send(self.part.at[at], self.summed.at[d, n], *self.sems(2, d, i), at_x(1 - 2 * d))

        def collect(self, i):
            n = self.slot(i)
            totals = []
            for d in range(2):
                wait_recv(self.raw.at[1 - d, n], self.sems(1, 1 - d, i)[1])
                wait_recv(self.summed.at[d, n], self.sems(2, d, i)[1])
                totals.append(self.part[self.at(x, i, d)] + self.raw[1 - d, n] + self.summed[d, n])
            return totals

    square_chunk, cube_chunk = rows // SQUARE, rows // CUBE
    square_sum = Sum(part1, relay1, raw1, summed1, rs1_send, rs1_recv, square_chunk)
    cube_sum = Sum(part2, relay2, raw2, summed2, rs2_send, rs2_recv, cube_chunk)

    def multiply_square(g, r):
        at = pl.ds(r * square_chunk, square_chunk)
        left = jnp.concatenate([a_ref[at, :], other[at, :]], axis=1)

        @pl.loop(0, 4, step=2)
        def _(p):
            right = jnp.concatenate(
                [jnp.concatenate([bt[h, g, p], bt[h, g, p + 1]], axis=1) for h in range(2)], axis=0
            )
            product = jnp.dot(left, right, preferred_element_type=F32)
            part1[g, p, at, :] = product[:, :cols]
            part1[g, p + 1, at, :] = product[:, cols:]

    def round_square(g, r):
        mid = square_chunk // 2
        for d, total in enumerate(square_sum.collect((g, r))):
            sb[g, yl, pl.ds((2 * r + d) * mid, mid), :] = total.astype(BF16)

    def slot_of(y_from, y_at):
        return rem(div(y_from, 4) + div(y_at, 4), 2) * 4 + rem(y_from, 4)

    def gather(g, r, s):
        mid = square_chunk // 2
        slots = GROUPS * SQUARE
        n = g * SQUARE + r

        def part(d, last):
            return pl.ds((2 * r + d) * mid, mid) if last else pl.ds(r * square_chunk, square_chunk)

        for d in range(2):
            sign = 1 - 2 * d
            y_from = rem(y + 8 - sign * s, 8)
            if s > 0:
                here = sb.at[g, slot_of(y_from, y), part(d, s == 4), :]
                wait_recv(here, ag_recv.at[(d * 5 + s) * slots + n])
            if s < 4:
                at = part(d, s == 3)
                y_to = rem(y + 8 + sign, 8)
                send(
                    sb.at[g, slot_of(y_from, y), at, :],
                    sb.at[g, slot_of(y_from, y_to), at, :],
                    ag_send.at[(d * 5 + s) * slots + n],
                    ag_recv.at[(d * 5 + s + 1) * slots + n],
                    at_y(sign),
                )

    def multiply_cube(r):
        at = pl.ds(r * cube_chunk, cube_chunk)
        left = jnp.concatenate([sb[g, s, at, :] for s in range(8) for g in range(GROUPS)], axis=1)

        @pl.loop(0, 4)
        def _(p):
            right = jnp.concatenate(
                [jnp.concatenate([bt[h, g, p] for g in range(GROUPS)], axis=1) for h in range(2)], axis=0
            )
            part2[p, at, :] = jnp.dot(left, right, preferred_element_type=F32)

    def purify(r):
        mid = cube_chunk // 2
        for d, total in enumerate(cube_sum.collect((None, r))):
            at = pl.ds((2 * r + d) * mid, mid)
            own = jnp.concatenate([sb[g, yl, at, :] for g in range(GROUPS)], axis=1).astype(F32)
            out_ref[at, :] = 3.0 * own - 2.0 * total

    events = []
    last = {}
    for g in range(GROUPS):
        begin = TICK * (2 * SPLIT * (5 if g == 0 else 8) + 4 * HOP)
        for r in range(SQUARE):
            t = begin + r * PERIOD
            if r == 0:
                events.append((t, lambda g=g: arrived(g)))
            events += [
                (t, lambda g=g, r=r: (multiply_square(g, r), square_sum.spread((g, r)))),
                (t + PASS, lambda g=g, r=r: square_sum.pass_on((g, r))),
                (t + COLLECT, lambda g=g, r=r: (round_square(g, r), gather(g, r, 0))),
            ]
            for s in range(1, 5):
                events.append((t + COLLECT + RING * s, lambda g=g, r=r, s=s: gather(g, r, s)))
            last[r] = t + COLLECT + RING * 4
    t = 0.0
    for r in range(CUBE):
        t = max(t + PERIOD_CUBE, last[(r + 1) * SQUARE // CUBE - 1])
        events += [
            (t, lambda r=r: (multiply_cube(r), cube_sum.spread((None, r)))),
            (t + PASS_CUBE, lambda r=r: cube_sum.pass_on((None, r))),
            (t + COLLECT_CUBE, lambda r=r: purify(r)),
        ]
    done = 0
    for t, event in sorted(events, key=lambda e: e[0]):
        due = min(TICKS, int(t / TICK))
        if due > done:
            pl.loop(done, due)(tick)
            done = due
        event()
    for wait in sent:
        wait()
    finish_operands()


def on_device(density):
    rows, width = density.shape
    share = width // 4
    cols = share // GROUPS
    dma = pltpu.SemaphoreType.DMA
    square_parts = pltpu.VMEM((2, GROUPS * SQUARE, rows // SQUARE // 2, cols), F32)
    cube_parts = pltpu.VMEM((2, CUBE, rows // CUBE // 2, share), F32)
    return pl.pallas_call(
        kernel,
        out_shape=jax.ShapeDtypeStruct((rows, share), F32),
        in_specs=[pl.BlockSpec(memory_space=pl.ANY)],
        out_specs=pl.BlockSpec(memory_space=pltpu.VMEM),
        scratch_shapes=[
            pltpu.VMEM((rows, width), BF16),
            pltpu.VMEM((GROUPS, rows, cols), BF16),
            pltpu.VMEM((rows, width), BF16),
            pltpu.VMEM((2, GROUPS, 4, 2 * rows, cols), BF16),
            pltpu.VMEM((GROUPS, 8, rows, cols), BF16),
            pltpu.VMEM((GROUPS, 4, rows, cols), F32),
            pltpu.VMEM((4, rows, share), F32),
            square_parts,
            square_parts,
            square_parts,
            cube_parts,
            cube_parts,
            cube_parts,
            dma((2 * SPLIT,)),
            dma((UNITS,)),
            dma((2 * STREAM,)),
            dma((2 * STREAM,)),
            dma((2 * UNITS,)),
            dma((2 * UNITS,)),
            dma((2 * UNITS,)),
            dma((2 * UNITS,)),
            dma((2 * UNITS,)),
            dma((UNITS,)),
            dma((UNITS,)),
            dma((2 * SPLIT,)),
            dma((GROUPS + 1,)),
            dma((6 * GROUPS * SQUARE,)),
            dma((6 * GROUPS * SQUARE,)),
            dma((6 * CUBE,)),
            dma((6 * CUBE,)),
            dma((10 * GROUPS * SQUARE,)),
            dma((10 * GROUPS * SQUARE,)),
        ],
        compiler_params=pltpu.CompilerParams(
            collective_id=0, has_side_effects=True, vmem_limit_bytes=48 * 1024 * 1024
        ),
    )(density)


def solution(mesh):
    return jax.shard_map(
        on_device, mesh=mesh, in_specs=(P("row", "col"),), out_specs=P("row", ("col", "depth")), check_vma=False
    )
```

```python
import jax
import jax.numpy as jnp
from jax import lax
from jax.experimental import pallas as pl
from jax.experimental.pallas import tpu as pltpu
from jax.sharding import PartitionSpec as P

MESH = pl.DeviceIdType.MESH
F32 = jnp.float32
BF16 = jnp.bfloat16

GROUPS = 2
SQUARE = 4
CUBE = 4
SPLIT = 2
UNITS = 8 * SPLIT
STREAM = 8 * SPLIT
HOP = 5
TICK = 0.75
TICKS = 2 * UNITS + 4 * HOP
ROWS = [TICK * (s + 4 * HOP) for s in (STREAM // 2, STREAM, STREAM // 2, STREAM)]
DOT = 0.4
PASS, COLLECT, RING, PERIOD = (0.7, 0.7), (4.4, 4.4), 3.5, 2.4
PASS_CUBE, NEAR_CUBE, COLLECT_CUBE, PERIOD_CUBE = 5.5, 10.0, 15.0, 2.0
QUIET = 13.5


def rem(a, b):
    return lax.rem(a, jnp.int32(b))


def div(a, b):
    return lax.div(a, jnp.int32(b))


def rel_half(z, yh):
    return rem(div(z, 4) + yh, 2)


def gray(e):
    return e + div(e, 2) * (5 - 2 * e)


def kernel(
    a_hbm, out_ref, a_ref, own, other, bt, sb, part1, part2, relay1, raw1, summed1, relay2, raw2, summed2,
    x_send, x_recv, y_send, y_recv, z_inject, z_forward, z_recv, cross_send, cross_recv, own_send, own_recv, own_local, load,
    rs1_send, rs1_recv, rs2_send, rs2_recv, ag_send, ag_recv,
):
    rows, width = a_hbm.shape
    share = width // 4
    cols = share // GROUPS
    row, col, yl = lax.axis_index("row"), lax.axis_index("col"), lax.axis_index("depth")
    z, core = div(row, 2), rem(row, 2)
    yh, x = div(col, 4), rem(col, 4)
    y = yh * 4 + yl

    def at_z(step, to_core):
        return (rem(z + 8 + step, 8) * 2 + to_core, col, yl)

    def at_y(step):
        to = rem(y + 8 + step, 8)
        return (row, div(to, 4) * 4 + x, rem(to, 4))

    def at_x(step):
        return (row, yh * 4 + rem(x + 4 + step, 4), yl)

    sibling = (z * 2 + 1 - core, col, yl)

    loads = [
        pltpu.make_async_copy(
            a_hbm.at[:, pl.ds(pl.multiple_of(yl * share + g * cols, cols), cols)], own.at[g], load.at[g]
        )
        for g in range(GROUPS)
    ] + [pltpu.make_async_copy(a_hbm, a_ref, load.at[GROUPS])]
    for copy in loads:
        copy.start()

    barrier = pltpu.get_barrier_semaphore()
    peers = [at_z(1, 0), at_z(1, 1), at_z(-1, 0), at_z(-1, 1), at_y(1), at_y(-1), at_x(1), at_x(-1), at_x(2), sibling]
    for peer in peers:
        pl.semaphore_signal(barrier, inc=1, device_id=peer, device_id_type=MESH)
    for copy in loads:
        copy.wait()
    pl.semaphore_wait(barrier, len(peers))

    def remote(src, dst, send, recv, device):
        return pltpu.make_async_remote_copy(
            src_ref=src, dst_ref=dst, send_sem=send, recv_sem=recv, device_id=device, device_id_type=MESH
        )

    def start(src, dst, send, recv, device):
        remote(src, dst, send, recv, device).start()

    def wait_recv(dst, sem):
        remote(dst, dst, sem, sem, sibling).wait_recv()

    def wait_send(src, sem):
        remote(src, src, sem, sem, sibling).wait_send()

    half = rows // 2
    strip = half // STREAM
    up = rem(z + 8 - x, 4)
    w = up + core * (rem(4 - up, 4) - up)
    is_source = w == 0
    away = w + 4 * (1 - lax.min(w, jnp.int32(1)))
    passed = rel_half(rem(z + 8 - (1 - 2 * core) * away, 8), yh)
    held = rel_half(z, yh)
    next_z = at_z(1 - 2 * core, core)

    unit = rows // SPLIT

    def tile(which, i, c):
        n, k = div(i, SPLIT), rem(i, SPLIT)
        u = div(n + 1, 3)
        others = lax.min(u, jnp.int32(1))
        g = others * (u - 1) + (1 - others) * n
        e = others * (rem(n, 3) + 1)
        at = pl.ds(pl.multiple_of(c * rows + k * unit, unit), unit)
        return bt.at[which, g, rem(x + gray(e), 4), at, :]

    def own_piece(g, k):
        return own.at[g, pl.ds(k * unit, unit), :]

    def own_copy(g, k):
        i = g * SPLIT + k
        return pltpu.make_async_copy(own_piece(g, k), tile(held, jnp.int32(i), core), own_local.at[i])

    def inject(i, src):
        dst = tile(held, i, core)
        m = i * 2 + core
        start(src, dst, z_inject.at[i], z_recv.at[m], at_z(1, 0))
        start(src, dst, z_inject.at[UNITS + i], z_recv.at[m], at_z(-1, 1))
        start(src, dst, own_send.at[i], own_recv.at[i], sibling)

    def passes(c):
        return (w > 0) & ((w < 3) | (c == core))

    def ring(m):
        i, c = div(m, 2), rem(m, 2)
        at = tile(passed, i, c)

        @pl.when((w > 0) | (c == core))
        def _():
            wait_recv(at, z_recv.at[m])

            @pl.when(passes(c))
            def _():
                start(at, at, z_forward.at[m], z_recv.at[m], next_z)

            start(at, at, cross_send.at[m], cross_recv.at[m], sibling)

    def strip_rows(d, j):
        return pl.ds(pl.multiple_of(d * half + j * strip, strip), strip)

    def stream(d, j):
        at = strip_rows(d, j)
        n = d * STREAM + j
        wait_recv(other.at[at, :], y_recv.at[n])

        @pl.when(yl != 3 * (1 - d))
        def _():
            start(other.at[at, :], other.at[at, :], y_send.at[n], y_recv.at[n], at_y(1 - 2 * d))

    @pl.when(is_source)
    def _():
        for g in range(GROUPS):
            for k in range(SPLIT):
                inject(jnp.int32(g * SPLIT + k), own_piece(g, k))
        for g in range(GROUPS):
            for k in range(SPLIT):
                own_copy(g, k).start()

    @pl.when(w > 0)
    def _():
        to = rem(z, 4)
        e = gray(rem(x + 4 - to, 4))
        for g in range(GROUPS):
            for k in range(SPLIT):
                dst = bt.at[held, g, x, pl.ds(pl.multiple_of(core * rows + k * unit, unit), unit), :]
                arrival = x_recv.at[(rem(e, 3) + 2 + 3 * g) * SPLIT + k]
                start(own_piece(g, k), dst, x_send.at[g * SPLIT + k], arrival, (row, yh * 4 + to, yl))

    for d in range(2):

        @pl.when(yl == 3 * (1 - d))
        def _():
            for j in range(STREAM):
                at = strip_rows(d, j)
                n = d * STREAM + j
                start(a_ref.at[at, :], other.at[at, :], y_send.at[n], y_recv.at[n], at_y(1 - 2 * d))

    def tick(t):
        i = t

        @pl.when(is_source & (i >= 2 * SPLIT) & (i < UNITS))
        def _():
            src = tile(held, i, core)
            wait_recv(src, x_recv.at[i])
            inject(i, src)

        m = t - HOP * away

        @pl.when((m >= 0) & (m < 2 * UNITS))
        def _():
            ring(m)

        for d in range(2):
            j = t - HOP * (yl + 1 if d == 0 else 4 - yl)

            @pl.when((j >= 0) & (j < STREAM))
            def _():
                stream(d, j)

    sib_w = rem(4 - w, 4)
    sib_away = sib_w + 4 * (1 - lax.min(sib_w, jnp.int32(1)))
    sib_passed = rel_half(rem(z + 8 + (1 - 2 * core) * sib_away, 8), yh)

    def arrived(g, b):
        first, after = [n * SPLIT for n in ((0, 3), (3, 5), (5, 6), (6, 8))[2 * g + b]]

        @pl.loop(2 * first, 2 * after)
        def _(m):
            i, c = div(m, 2), rem(m, 2)

            @pl.when((w > 0) | (c != core))
            def _():
                wait_recv(tile(sib_passed, i, c), cross_recv.at[m])

        @pl.when(is_source)
        def _():
            if g == 0 and b == 0:
                for i in range(2 * SPLIT):
                    own_copy(i // SPLIT, i % SPLIT).wait()

            @pl.loop(first, after)
            def _(i):
                wait_recv(tile(held, i, 1 - core), own_recv.at[i])

    def finish_operands():
        @pl.when(w > 0)
        def _():
            for i in range(2 * SPLIT):
                wait_send(bt.at[held, 0, x, pl.ds(0, unit), :], x_send.at[i])

        @pl.when(is_source)
        def _():
            @pl.loop(0, UNITS)
            def _(i):
                src = tile(held, i, core)
                wait_send(src, z_inject.at[i])
                wait_send(src, z_inject.at[UNITS + i])
                wait_send(src, own_send.at[i])

        @pl.loop(0, 2 * UNITS)
        def _(m):
            i, c = div(m, 2), rem(m, 2)
            at = tile(passed, i, c)

            @pl.when((w > 0) | (c == core))
            def _():
                wait_send(at, cross_send.at[m])

                @pl.when(passes(c))
                def _():
                    wait_send(at, z_forward.at[m])

        @pl.loop(0, 2 * STREAM)
        def _(n):
            at = pl.ds(pl.multiple_of(n * strip, strip), strip)
            wait_send(other.at[at, :], y_send.at[n])

    ahead, behind, across = rem(x + 1, 4), rem(x + 3, 4), rem(x + 2, 4)
    sent = []

    def send(src, dst, send_sem, recv_sem, device):
        copy = remote(src, dst, send_sem, recv_sem, device)
        copy.start()
        sent.append(copy.wait_send)

    class Sum:
        def __init__(self, part, relay, raw, summed, sends, recvs, chunk):
            self.part, self.relay, self.raw, self.summed = part, relay, raw, summed
            self.sends, self.recvs, self.mid = sends, recvs, chunk // 2
            self.slots = relay.shape[1]

        def at(self, piece, i, which):
            g, r = i
            rows_at = pl.ds((2 * r + which) * self.mid, self.mid)
            return (g, piece, rows_at, slice(None)) if g is not None else (piece, rows_at, slice(None))

        def slot(self, i):
            return i[0] * SQUARE + i[1] if i[0] is not None else i[1]

        def sems(self, kind, d, i):
            n = (kind * 2 + d) * self.slots + self.slot(i)
            return self.sends.at[n], self.recvs.at[n]

        def spread_far(self, i):
            n = self.slot(i)
            for d in range(2):
                src = self.part.at[self.at(across, i, d)]
                send(src, self.relay.at[d, n], *self.sems(0, d, i), at_x(1 - 2 * d))

        def spread_near(self, i):
            n = self.slot(i)
            for d in range(2):
                src = self.part.at[self.at(ahead if d == 0 else behind, i, 1 - d)]
                send(src, self.raw.at[d, n], *self.sems(1, d, i), at_x(1 - 2 * d))

        def pass_on(self, i):
            n = self.slot(i)
            for d in range(2):
                wait_recv(self.relay.at[d, n], self.sems(0, d, i)[1])
                at = self.at(ahead if d == 0 else behind, i, d)
                self.part[at] = self.part[at] + self.relay[d, n]
                send(self.part.at[at], self.summed.at[d, n], *self.sems(2, d, i), at_x(1 - 2 * d))

        def collect(self, i):
            n = self.slot(i)
            totals = []
            for d in range(2):
                wait_recv(self.raw.at[1 - d, n], self.sems(1, 1 - d, i)[1])
                wait_recv(self.summed.at[d, n], self.sems(2, d, i)[1])
                totals.append(self.part[self.at(x, i, d)] + self.raw[1 - d, n] + self.summed[d, n])
            return totals

    square_chunk, cube_chunk = rows // SQUARE, rows // CUBE
    square_sum = Sum(part1, relay1, raw1, summed1, rs1_send, rs1_recv, square_chunk)
    cube_sum = Sum(part2, relay2, raw2, summed2, rs2_send, rs2_recv, cube_chunk)

    def multiply_square(g, r, b):
        at = pl.ds(r * square_chunk, square_chunk)
        left = jnp.concatenate([a_ref[at, :], other[at, :]], axis=1)
        p, q = rem(x + b, 4), rem(x + b + 2, 4)
        right = jnp.concatenate([jnp.concatenate([bt[h, g, p], bt[h, g, q]], axis=1) for h in range(2)], axis=0)
        product = jnp.dot(left, right, preferred_element_type=F32)
        part1[g, p, at, :] = product[:, :cols]
        part1[g, q, at, :] = product[:, cols:]

    def round_square(g, r):
        mid = square_chunk // 2
        for d, total in enumerate(square_sum.collect((g, r))):
            sb[g, yl, pl.ds((2 * r + d) * mid, mid), :] = total.astype(BF16)

    def slot_of(y_from, y_at):
        return rem(div(y_from, 4) + div(y_at, 4), 2) * 4 + rem(y_from, 4)

    def gather(g, r, s):
        mid = square_chunk // 2
        slots = GROUPS * SQUARE
        n = g * SQUARE + r

        def part(d, last):
            return pl.ds((2 * r + d) * mid, mid) if last else pl.ds(r * square_chunk, square_chunk)

        for d in range(2):
            sign = 1 - 2 * d
            y_from = rem(y + 8 - sign * s, 8)
            if s > 0:
                here = sb.at[g, slot_of(y_from, y), part(d, s == 4), :]
                wait_recv(here, ag_recv.at[(d * 5 + s) * slots + n])
            if s < 4:
                at = part(d, s == 3)
                y_to = rem(y + 8 + sign, 8)
                send(
                    sb.at[g, slot_of(y_from, y), at, :],
                    sb.at[g, slot_of(y_from, y_to), at, :],
                    ag_send.at[(d * 5 + s) * slots + n],
                    ag_recv.at[(d * 5 + s + 1) * slots + n],
                    at_y(sign),
                )

    def multiply_cube(r):
        at = pl.ds(r * cube_chunk, cube_chunk)
        left = jnp.concatenate([sb[g, s, at, :] for s in range(8) for g in range(GROUPS)], axis=1)

        @pl.loop(0, 4)
        def _(p):
            right = jnp.concatenate(
                [jnp.concatenate([bt[h, g, p] for g in range(GROUPS)], axis=1) for h in range(2)], axis=0
            )
            part2[p, at, :] = jnp.dot(left, right, preferred_element_type=F32)

    def purify(r):
        mid = cube_chunk // 2
        for d, total in enumerate(cube_sum.collect((None, r))):
            at = pl.ds((2 * r + d) * mid, mid)
            own = jnp.concatenate([sb[g, yl, at, :] for g in range(GROUPS)], axis=1).astype(F32)
            out_ref[at, :] = 3.0 * own - 2.0 * total

    events, square_sends = [], []
    last = {}
    for g in range(GROUPS):
        begin, whole = [TICK * (2 * SPLIT * n + 4 * HOP) for n in ((3, 5), (6, 8))[g]]
        events += [(begin, lambda g=g: arrived(g, 0)), (whole, lambda g=g: arrived(g, 1))]
        for r in range(SQUARE):
            t = max(begin, ROWS[r * 4 // SQUARE] if g == 0 else 0) + r * DOT
            events.append((t, lambda g=g, r=r: (multiply_square(g, r, 0), square_sum.spread_far((g, r)))))
            t = whole + r * PERIOD
            events += [
                (t, lambda g=g, r=r: multiply_square(g, r, 1)),
                (t + PASS[g], lambda g=g, r=r: square_sum.pass_on((g, r))),
                (t + PASS[g], lambda g=g, r=r: square_sum.spread_near((g, r))),
                (t + COLLECT[g], lambda g=g, r=r: (round_square(g, r), gather(g, r, 0))),
            ]
            for s in range(1, 5):
                events.append((t + COLLECT[g] + RING * s, lambda g=g, r=r, s=s: gather(g, r, s)))
            last[r] = t + COLLECT[g] + RING * 4
    t = 0.0
    for r in range(CUBE):
        t = max(t + PERIOD, last[((r + 1) * SQUARE - 1) // CUBE])
        if r == 0:
            first = t
            events.append((first + QUIET, lambda: finish_operands()))
            events.append((first - 0.01, lambda: (square_sends.extend(sent), sent.clear())))
            events.append((first + QUIET, lambda: [wait() for wait in square_sends]))
        events += [
            (t, lambda r=r: (multiply_cube(r), cube_sum.spread_far((None, r)))),
            (t + PASS_CUBE, lambda r=r: cube_sum.pass_on((None, r))),
            (t if r == 0 else first + NEAR_CUBE + r * PERIOD_CUBE, lambda r=r: cube_sum.spread_near((None, r))),
            (first + COLLECT_CUBE + r * PERIOD_CUBE, lambda r=r: purify(r)),
        ]
    done = 0
    for t, event in sorted(events, key=lambda e: e[0]):
        due = min(TICKS, int(t / TICK))
        if due > done:
            pl.loop(done, due)(tick)
            done = due
        event()
    for wait in sent:
        wait()


def on_device(density):
    rows, width = density.shape
    share = width // 4
    cols = share // GROUPS
    dma = pltpu.SemaphoreType.DMA
    square_parts = pltpu.VMEM((2, GROUPS * SQUARE, rows // SQUARE // 2, cols), F32)
    cube_parts = pltpu.VMEM((2, CUBE, rows // CUBE // 2, share), F32)
    return pl.pallas_call(
        kernel,
        out_shape=jax.ShapeDtypeStruct((rows, share), F32),
        in_specs=[pl.BlockSpec(memory_space=pl.ANY)],
        out_specs=pl.BlockSpec(memory_space=pltpu.VMEM),
        scratch_shapes=[
            pltpu.VMEM((rows, width), BF16),
            pltpu.VMEM((GROUPS, rows, cols), BF16),
            pltpu.VMEM((rows, width), BF16),
            pltpu.VMEM((2, GROUPS, 4, 2 * rows, cols), BF16),
            pltpu.VMEM((GROUPS, 8, rows, cols), BF16),
            pltpu.VMEM((GROUPS, 4, rows, cols), F32),
            pltpu.VMEM((4, rows, share), F32),
            square_parts,
            square_parts,
            square_parts,
            cube_parts,
            cube_parts,
            cube_parts,
            dma((2 * SPLIT,)),
            dma((UNITS,)),
            dma((2 * STREAM,)),
            dma((2 * STREAM,)),
            dma((2 * UNITS,)),
            dma((2 * UNITS,)),
            dma((2 * UNITS,)),
            dma((2 * UNITS,)),
            dma((2 * UNITS,)),
            dma((UNITS,)),
            dma((UNITS,)),
            dma((2 * SPLIT,)),
            dma((GROUPS + 1,)),
            dma((6 * GROUPS * SQUARE,)),
            dma((6 * GROUPS * SQUARE,)),
            dma((6 * CUBE,)),
            dma((6 * CUBE,)),
            dma((10 * GROUPS * SQUARE,)),
            dma((10 * GROUPS * SQUARE,)),
        ],
        compiler_params=pltpu.CompilerParams(
            collective_id=0, has_side_effects=True, vmem_limit_bytes=48 * 1024 * 1024
        ),
    )(density)


def solution(mesh):
    return jax.shard_map(
        on_device, mesh=mesh, in_specs=(P("row", "col"),), out_specs=P("row", ("col", "depth")), check_vma=False
    )
```

```python
import jax
import jax.numpy as jnp
from jax import lax
from jax.experimental import pallas as pl
from jax.experimental.pallas import tpu as pltpu
from jax.sharding import PartitionSpec as P

MESH = pl.DeviceIdType.MESH
F32 = jnp.float32
BF16 = jnp.bfloat16

GROUPS = 2
SQUARE = 4
CUBE = 4
SPLIT = 2
UNITS = 8 * SPLIT
STREAM = 8 * SPLIT
HOP = 5
TICK = 0.75
TICKS = 2 * UNITS + 4 * HOP
ROWS = [TICK * (s + 4 * HOP) for s in (STREAM // 2, STREAM, STREAM // 2, STREAM)]
DOT = 0.4
PASS, COLLECT, RING, PERIOD = (0.7, 0.7), (4.4, 4.4), 3.5, 2.4
PASS_CUBE, NEAR_CUBE, COLLECT_CUBE, PERIOD_CUBE = 5.5, 10.0, 15.0, 2.0
QUIET = 13.5


def rem(a, b):
    return lax.rem(a, jnp.int32(b))


def div(a, b):
    return lax.div(a, jnp.int32(b))


def rel_half(z, yh):
    return rem(div(z, 4) + yh, 2)


def gray(e):
    return e + div(e, 2) * (5 - 2 * e)


def kernel(
    a_hbm, out_ref, a_ref, own, other, bt, sb, part1, part2, relay1, raw1, summed1, relay2, raw2, summed2,
    x_send, x_recv, y_send, y_recv, z_inject, z_forward, z_recv, cross_send, cross_recv, own_send, own_recv, own_local, load,
    rs1_send, rs1_recv, rs2_send, rs2_recv, ag_send, ag_recv,
):
    rows, width = a_hbm.shape
    share = width // 4
    cols = share // GROUPS
    row, col, yl = lax.axis_index("row"), lax.axis_index("col"), lax.axis_index("depth")
    z, core = div(row, 2), rem(row, 2)
    yh, x = div(col, 4), rem(col, 4)
    y = yh * 4 + yl

    def at_z(step, to_core):
        return (rem(z + 8 + step, 8) * 2 + to_core, col, yl)

    def at_y(step):
        to = rem(y + 8 + step, 8)
        return (row, div(to, 4) * 4 + x, rem(to, 4))

    def at_x(step):
        return (row, yh * 4 + rem(x + 4 + step, 4), yl)

    sibling = (z * 2 + 1 - core, col, yl)

    loads = [
        pltpu.make_async_copy(
            a_hbm.at[:, pl.ds(pl.multiple_of(yl * share + g * cols, cols), cols)], own.at[g], load.at[g]
        )
        for g in range(GROUPS)
    ] + [pltpu.make_async_copy(a_hbm, a_ref, load.at[GROUPS])]
    for copy in loads:
        copy.start()

    barrier = pltpu.get_barrier_semaphore()
    peers = [at_z(1, 0), at_z(1, 1), at_z(-1, 0), at_z(-1, 1), at_y(1), at_y(-1), at_x(1), at_x(-1), at_x(2), sibling]
    for peer in peers:
        pl.semaphore_signal(barrier, inc=1, device_id=peer, device_id_type=MESH)
    for copy in loads:
        copy.wait()
    pl.semaphore_wait(barrier, len(peers))

    def remote(src, dst, send, recv, device):
        return pltpu.make_async_remote_copy(
            src_ref=src, dst_ref=dst, send_sem=send, recv_sem=recv, device_id=device, device_id_type=MESH
        )

    def start(src, dst, send, recv, device):
        remote(src, dst, send, recv, device).start()

    def wait_recv(dst, sem):
        remote(dst, dst, sem, sem, sibling).wait_recv()

    def wait_send(src, sem):
        remote(src, src, sem, sem, sibling).wait_send()

    half = rows // 2
    strip = half // STREAM
    up = rem(z + 8 - x, 4)
    w = up + core * (rem(4 - up, 4) - up)
    is_source = w == 0
    away = w + 4 * (1 - lax.min(w, jnp.int32(1)))
    passed = rel_half(rem(z + 8 - (1 - 2 * core) * away, 8), yh)
    held = rel_half(z, yh)
    next_z = at_z(1 - 2 * core, core)

    unit = rows // SPLIT

    def tile(which, i, c):
        n, k = div(i, SPLIT), rem(i, SPLIT)
        u = div(n + 1, 3)
        others = lax.min(u, jnp.int32(1))
        g = others * (u - 1) + (1 - others) * n
        e = others * (rem(n, 3) + 1)
        at = pl.ds(pl.multiple_of(c * rows + k * unit, unit), unit)
        return bt.at[which, g, rem(x + gray(e), 4), at, :]

    def own_piece(g, k):
        return own.at[g, pl.ds(k * unit, unit), :]

    def own_copy(g, k):
        i = g * SPLIT + k
        return pltpu.make_async_copy(own_piece(g, k), tile(held, jnp.int32(i), core), own_local.at[i])

    def inject(i, src):
        dst = tile(held, i, core)
        m = i * 2 + core
        start(src, dst, z_inject.at[i], z_recv.at[m], at_z(1, 0))
        start(src, dst, z_inject.at[UNITS + i], z_recv.at[m], at_z(-1, 1))
        start(src, dst, own_send.at[i], own_recv.at[i], sibling)

    def passes(c):
        return (w > 0) & ((w < 3) | (c == core))

    def ring(m):
        i, c = div(m, 2), rem(m, 2)
        at = tile(passed, i, c)

        @pl.when((w > 0) | (c == core))
        def _():
            wait_recv(at, z_recv.at[m])

            @pl.when(passes(c))
            def _():
                start(at, at, z_forward.at[m], z_recv.at[m], next_z)

            start(at, at, cross_send.at[m], cross_recv.at[m], sibling)

    def strip_rows(d, j):
        return pl.ds(pl.multiple_of(d * half + j * strip, strip), strip)

    def stream(d, j):
        at = strip_rows(d, j)
        n = d * STREAM + j
        wait_recv(other.at[at, :], y_recv.at[n])

        @pl.when(yl != 3 * (1 - d))
        def _():
            start(other.at[at, :], other.at[at, :], y_send.at[n], y_recv.at[n], at_y(1 - 2 * d))

    @pl.when(is_source)
    def _():
        for g in range(GROUPS):
            for k in range(SPLIT):
                inject(jnp.int32(g * SPLIT + k), own_piece(g, k))
        for g in range(GROUPS):
            for k in range(SPLIT):
                own_copy(g, k).start()

    @pl.when(w > 0)
    def _():
        to = rem(z, 4)
        e = gray(rem(x + 4 - to, 4))
        for g in range(GROUPS):
            for k in range(SPLIT):
                dst = bt.at[held, g, x, pl.ds(pl.multiple_of(core * rows + k * unit, unit), unit), :]
                arrival = x_recv.at[(rem(e, 3) + 2 + 3 * g) * SPLIT + k]
                start(own_piece(g, k), dst, x_send.at[g * SPLIT + k], arrival, (row, yh * 4 + to, yl))

    for d in range(2):

        @pl.when(yl == 3 * (1 - d))
        def _():
            for j in range(STREAM):
                at = strip_rows(d, j)
                n = d * STREAM + j
                start(a_ref.at[at, :], other.at[at, :], y_send.at[n], y_recv.at[n], at_y(1 - 2 * d))

    def tick(t):
        i = t - 3

        @pl.when(is_source & (i >= 2 * SPLIT) & (i < UNITS))
        def _():
            src = tile(held, i, core)
            wait_recv(src, x_recv.at[i])
            inject(i, src)

        m = t - 4 * away

        @pl.when((m >= 0) & (m < 2 * UNITS))
        def _():
            ring(m)

        for d in range(2):
            j = t - HOP * (yl + 1 if d == 0 else 4 - yl)

            @pl.when((j >= 0) & (j < STREAM))
            def _():
                stream(d, j)

    sib_w = rem(4 - w, 4)
    sib_away = sib_w + 4 * (1 - lax.min(sib_w, jnp.int32(1)))
    sib_passed = rel_half(rem(z + 8 + (1 - 2 * core) * sib_away, 8), yh)

    def arrived(g, b):
        first, after = [n * SPLIT for n in ((0, 3), (3, 5), (5, 6), (6, 8))[2 * g + b]]

        @pl.loop(2 * first, 2 * after)
        def _(m):
            i, c = div(m, 2), rem(m, 2)

            @pl.when((w > 0) | (c != core))
            def _():
                wait_recv(tile(sib_passed, i, c), cross_recv.at[m])

        @pl.when(is_source)
        def _():
            if g == 0 and b == 0:
                for i in range(2 * SPLIT):
                    own_copy(i // SPLIT, i % SPLIT).wait()

            @pl.loop(first, after)
            def _(i):
                wait_recv(tile(held, i, 1 - core), own_recv.at[i])

    def finish_operands():
        @pl.when(w > 0)
        def _():
            for i in range(2 * SPLIT):
                wait_send(bt.at[held, 0, x, pl.ds(0, unit), :], x_send.at[i])

        @pl.when(is_source)
        def _():
            @pl.loop(0, UNITS)
            def _(i):
                src = tile(held, i, core)
                wait_send(src, z_inject.at[i])
                wait_send(src, z_inject.at[UNITS + i])
                wait_send(src, own_send.at[i])

        @pl.loop(0, 2 * UNITS)
        def _(m):
            i, c = div(m, 2), rem(m, 2)
            at = tile(passed, i, c)

            @pl.when((w > 0) | (c == core))
            def _():
                wait_send(at, cross_send.at[m])

                @pl.when(passes(c))
                def _():
                    wait_send(at, z_forward.at[m])

        @pl.loop(0, 2 * STREAM)
        def _(n):
            at = pl.ds(pl.multiple_of(n * strip, strip), strip)
            wait_send(other.at[at, :], y_send.at[n])

    ahead, behind, across = rem(x + 1, 4), rem(x + 3, 4), rem(x + 2, 4)
    sent = []

    def send(src, dst, send_sem, recv_sem, device):
        copy = remote(src, dst, send_sem, recv_sem, device)
        copy.start()
        sent.append(copy.wait_send)

    class Sum:
        def __init__(self, part, relay, raw, summed, sends, recvs, chunk):
            self.part, self.relay, self.raw, self.summed = part, relay, raw, summed
            self.sends, self.recvs, self.mid = sends, recvs, chunk // 2
            self.slots = relay.shape[1]

        def at(self, piece, i, which):
            g, r = i
            rows_at = pl.ds((2 * r + which) * self.mid, self.mid)
            return (g, piece, rows_at, slice(None)) if g is not None else (piece, rows_at, slice(None))

        def slot(self, i):
            return i[0] * SQUARE + i[1] if i[0] is not None else i[1]

        def sems(self, kind, d, i):
            n = (kind * 2 + d) * self.slots + self.slot(i)
            return self.sends.at[n], self.recvs.at[n]

        def spread_far(self, i):
            n = self.slot(i)
            for d in range(2):
                src = self.part.at[self.at(across, i, d)]
                send(src, self.relay.at[d, n], *self.sems(0, d, i), at_x(1 - 2 * d))

        def spread_near(self, i):
            n = self.slot(i)
            for d in range(2):
                src = self.part.at[self.at(ahead if d == 0 else behind, i, 1 - d)]
                send(src, self.raw.at[d, n], *self.sems(1, d, i), at_x(1 - 2 * d))

        def pass_on(self, i):
            n = self.slot(i)
            for d in range(2):
                wait_recv(self.relay.at[d, n], self.sems(0, d, i)[1])
                at = self.at(ahead if d == 0 else behind, i, d)
                self.part[at] = self.part[at] + self.relay[d, n]
                send(self.part.at[at], self.summed.at[d, n], *self.sems(2, d, i), at_x(1 - 2 * d))

        def collect(self, i):
            n = self.slot(i)
            totals = []
            for d in range(2):
                wait_recv(self.raw.at[1 - d, n], self.sems(1, 1 - d, i)[1])
                wait_recv(self.summed.at[d, n], self.sems(2, d, i)[1])
                totals.append(self.part[self.at(x, i, d)] + self.raw[1 - d, n] + self.summed[d, n])
            return totals

    square_chunk, cube_chunk = rows // SQUARE, rows // CUBE
    square_sum = Sum(part1, relay1, raw1, summed1, rs1_send, rs1_recv, square_chunk)
    cube_sum = Sum(part2, relay2, raw2, summed2, rs2_send, rs2_recv, cube_chunk)

    def multiply_square(g, r, b):
        at = pl.ds(r * square_chunk, square_chunk)
        left = jnp.concatenate([a_ref[at, :], other[at, :]], axis=1)
        p, q = rem(x + b, 4), rem(x + b + 2, 4)
        right = jnp.concatenate([jnp.concatenate([bt[h, g, p], bt[h, g, q]], axis=1) for h in range(2)], axis=0)
        product = jnp.dot(left, right, preferred_element_type=F32)
        part1[g, p, at, :] = product[:, :cols]
        part1[g, q, at, :] = product[:, cols:]

    def round_square(g, r):
        mid = square_chunk // 2
        for d, total in enumerate(square_sum.collect((g, r))):
            sb[g, yl, pl.ds((2 * r + d) * mid, mid), :] = total.astype(BF16)

    def slot_of(y_from, y_at):
        return rem(div(y_from, 4) + div(y_at, 4), 2) * 4 + rem(y_from, 4)

    def gather(g, r, s):
        mid = square_chunk // 2
        slots = GROUPS * SQUARE
        n = g * SQUARE + r

        def part(d, last):
            return pl.ds((2 * r + d) * mid, mid) if last else pl.ds(r * square_chunk, square_chunk)

        for d in range(2):
            sign = 1 - 2 * d
            y_from = rem(y + 8 - sign * s, 8)
            if s > 0:
                here = sb.at[g, slot_of(y_from, y), part(d, s == 4), :]
                wait_recv(here, ag_recv.at[(d * 5 + s) * slots + n])
            if s < 4:
                at = part(d, s == 3)
                y_to = rem(y + 8 + sign, 8)
                send(
                    sb.at[g, slot_of(y_from, y), at, :],
                    sb.at[g, slot_of(y_from, y_to), at, :],
                    ag_send.at[(d * 5 + s) * slots + n],
                    ag_recv.at[(d * 5 + s + 1) * slots + n],
                    at_y(sign),
                )

    def multiply_cube(r):
        at = pl.ds(r * cube_chunk, cube_chunk)
        left = jnp.concatenate([sb[g, s, at, :] for s in range(8) for g in range(GROUPS)], axis=1)

        @pl.loop(0, 4)
        def _(p):
            right = jnp.concatenate(
                [jnp.concatenate([bt[h, g, p] for g in range(GROUPS)], axis=1) for h in range(2)], axis=0
            )
            part2[p, at, :] = jnp.dot(left, right, preferred_element_type=F32)

    def purify(r):
        mid = cube_chunk // 2
        for d, total in enumerate(cube_sum.collect((None, r))):
            at = pl.ds((2 * r + d) * mid, mid)
            own = jnp.concatenate([sb[g, yl, at, :] for g in range(GROUPS)], axis=1).astype(F32)
            out_ref[at, :] = 3.0 * own - 2.0 * total

    events, square_sends = [], []
    last = {}
    for g in range(GROUPS):
        begin, whole = [TICK * (2 * SPLIT * n + 4 * HOP) for n in ((3, 5), (6, 8))[g]]
        events += [(begin, lambda g=g: arrived(g, 0)), (whole, lambda g=g: arrived(g, 1))]
        for r in range(SQUARE):
            t = max(begin, ROWS[r * 4 // SQUARE] if g == 0 else 0) + r * DOT
            events.append((t, lambda g=g, r=r: (multiply_square(g, r, 0), square_sum.spread_far((g, r)))))
            t = whole + r * PERIOD
            events += [
                (t, lambda g=g, r=r: multiply_square(g, r, 1)),
                (t + PASS[g], lambda g=g, r=r: square_sum.pass_on((g, r))),
                (t + PASS[g], lambda g=g, r=r: square_sum.spread_near((g, r))),
                (t + COLLECT[g], lambda g=g, r=r: (round_square(g, r), gather(g, r, 0))),
            ]
            for s in range(1, 5):
                events.append((t + COLLECT[g] + RING * s, lambda g=g, r=r, s=s: gather(g, r, s)))
            last[r] = t + COLLECT[g] + RING * 4
    t = 0.0
    for r in range(CUBE):
        t = max(t + PERIOD, last[((r + 1) * SQUARE - 1) // CUBE])
        if r == 0:
            first = t
            events.append((first + QUIET, lambda: finish_operands()))
            events.append((first - 0.01, lambda: (square_sends.extend(sent), sent.clear())))
            events.append((first + QUIET, lambda: [wait() for wait in square_sends]))
        events += [
            (t, lambda r=r: (multiply_cube(r), cube_sum.spread_far((None, r)))),
            (t + PASS_CUBE, lambda r=r: cube_sum.pass_on((None, r))),
            (t if r == 0 else first + NEAR_CUBE + r * PERIOD_CUBE, lambda r=r: cube_sum.spread_near((None, r))),
            (first + COLLECT_CUBE + r * PERIOD_CUBE, lambda r=r: purify(r)),
        ]
    done = 0
    for t, event in sorted(events, key=lambda e: e[0]):
        due = min(TICKS, int(t / TICK))
        if due > done:
            pl.loop(done, due)(tick)
            done = due
        event()
    for wait in sent:
        wait()


def on_device(density):
    rows, width = density.shape
    share = width // 4
    cols = share // GROUPS
    dma = pltpu.SemaphoreType.DMA
    square_parts = pltpu.VMEM((2, GROUPS * SQUARE, rows // SQUARE // 2, cols), F32)
    cube_parts = pltpu.VMEM((2, CUBE, rows // CUBE // 2, share), F32)
    return pl.pallas_call(
        kernel,
        out_shape=jax.ShapeDtypeStruct((rows, share), F32),
        in_specs=[pl.BlockSpec(memory_space=pl.ANY)],
        out_specs=pl.BlockSpec(memory_space=pltpu.VMEM),
        scratch_shapes=[
            pltpu.VMEM((rows, width), BF16),
            pltpu.VMEM((GROUPS, rows, cols), BF16),
            pltpu.VMEM((rows, width), BF16),
            pltpu.VMEM((2, GROUPS, 4, 2 * rows, cols), BF16),
            pltpu.VMEM((GROUPS, 8, rows, cols), BF16),
            pltpu.VMEM((GROUPS, 4, rows, cols), F32),
            pltpu.VMEM((4, rows, share), F32),
            square_parts,
            square_parts,
            square_parts,
            cube_parts,
            cube_parts,
            cube_parts,
            dma((2 * SPLIT,)),
            dma((UNITS,)),
            dma((2 * STREAM,)),
            dma((2 * STREAM,)),
            dma((2 * UNITS,)),
            dma((2 * UNITS,)),
            dma((2 * UNITS,)),
            dma((2 * UNITS,)),
            dma((2 * UNITS,)),
            dma((UNITS,)),
            dma((UNITS,)),
            dma((2 * SPLIT,)),
            dma((GROUPS + 1,)),
            dma((6 * GROUPS * SQUARE,)),
            dma((6 * GROUPS * SQUARE,)),
            dma((6 * CUBE,)),
            dma((6 * CUBE,)),
            dma((10 * GROUPS * SQUARE,)),
            dma((10 * GROUPS * SQUARE,)),
        ],
        compiler_params=pltpu.CompilerParams(
            collective_id=0, has_side_effects=True, vmem_limit_bytes=48 * 1024 * 1024
        ),
    )(density)


def solution(mesh):
    return jax.shard_map(
        on_device, mesh=mesh, in_specs=(P("row", "col"),), out_specs=P("row", ("col", "depth")), check_vma=False
    )
```

```python
import jax
import jax.numpy as jnp
from jax import lax
from jax.experimental import pallas as pl
from jax.experimental.pallas import tpu as pltpu
from jax.sharding import PartitionSpec as P

MESH = pl.DeviceIdType.MESH
F32 = jnp.float32
BF16 = jnp.bfloat16

GROUPS = 2
SQUARE = 4
CUBE = 4
SPLIT = 2
UNITS = 8 * SPLIT
STREAM = 8 * SPLIT
HOP = 5
TICK = 0.75
TICKS = 2 * UNITS + 4 * HOP
ROWS = [TICK * (s + 4 * HOP) for s in (STREAM // 2, STREAM, STREAM // 2, STREAM)]
DOT = 0.4
PASS, COLLECT, RING, PERIOD = (0.7, 0.7), (4.4, 4.4), 3.5, 2.4
PASS_CUBE, NEAR_CUBE, COLLECT_CUBE, PERIOD_CUBE = 5.5, 10.0, 15.0, 2.0
QUIET = 13.5


def rem(a, b):
    return lax.rem(a, jnp.int32(b))


def div(a, b):
    return lax.div(a, jnp.int32(b))


def rel_half(z, yh):
    return rem(div(z, 4) + yh, 2)


def gray(e):
    return e + div(e, 2) * (5 - 2 * e)


def kernel(
    a_hbm, out_ref, a_ref, own, other, bt, sb, part1, part2, relay1, raw1, summed1, relay2, raw2, summed2,
    x_send, x_recv, y_send, y_recv, z_inject, z_forward, z_recv, cross_send, cross_recv, own_send, own_recv, own_local, load,
    rs1_send, rs1_recv, rs2_send, rs2_recv, ag_send, ag_recv,
):
    rows, width = a_hbm.shape
    share = width // 4
    cols = share // GROUPS
    row, col, yl = lax.axis_index("row"), lax.axis_index("col"), lax.axis_index("depth")
    z, core = div(row, 2), rem(row, 2)
    yh, x = div(col, 4), rem(col, 4)
    y = yh * 4 + yl

    def at_z(step, to_core):
        return (rem(z + 8 + step, 8) * 2 + to_core, col, yl)

    def at_y(step):
        to = rem(y + 8 + step, 8)
        return (row, div(to, 4) * 4 + x, rem(to, 4))

    def at_x(step):
        return (row, yh * 4 + rem(x + 4 + step, 4), yl)

    sibling = (z * 2 + 1 - core, col, yl)

    loads = [
        pltpu.make_async_copy(
            a_hbm.at[:, pl.ds(pl.multiple_of(yl * share + g * cols, cols), cols)], own.at[g], load.at[g]
        )
        for g in range(GROUPS)
    ] + [pltpu.make_async_copy(a_hbm, a_ref, load.at[GROUPS])]
    for copy in loads:
        copy.start()

    barrier = pltpu.get_barrier_semaphore()
    peers = [at_z(1, 0), at_z(1, 1), at_z(-1, 0), at_z(-1, 1), at_y(1), at_y(-1), at_x(1), at_x(-1), at_x(2), sibling]
    for peer in peers:
        pl.semaphore_signal(barrier, inc=1, device_id=peer, device_id_type=MESH)
    for copy in loads:
        copy.wait()
    pl.semaphore_wait(barrier, len(peers))

    def remote(src, dst, send, recv, device):
        return pltpu.make_async_remote_copy(
            src_ref=src, dst_ref=dst, send_sem=send, recv_sem=recv, device_id=device, device_id_type=MESH
        )

    def start(src, dst, send, recv, device):
        remote(src, dst, send, recv, device).start()

    def wait_recv(dst, sem):
        remote(dst, dst, sem, sem, sibling).wait_recv()

    def wait_send(src, sem):
        remote(src, src, sem, sem, sibling).wait_send()

    half = rows // 2
    strip = half // STREAM
    up = rem(z + 8 - x, 4)
    w = up + core * (rem(4 - up, 4) - up)
    is_source = w == 0
    away = w + 4 * (1 - lax.min(w, jnp.int32(1)))
    passed = rel_half(rem(z + 8 - (1 - 2 * core) * away, 8), yh)
    held = rel_half(z, yh)
    next_z = at_z(1 - 2 * core, core)

    unit = rows // SPLIT

    def tile(which, i, c):
        n, k = div(i, SPLIT), rem(i, SPLIT)
        u = div(n + 1, 3)
        others = lax.min(u, jnp.int32(1))
        g = others * (u - 1) + (1 - others) * n
        e = others * (rem(n, 3) + 1)
        at = pl.ds(pl.multiple_of(c * rows + k * unit, unit), unit)
        return bt.at[which, g, rem(x + gray(e), 4), at, :]

    def own_piece(g, k):
        return own.at[g, pl.ds(k * unit, unit), :]

    def own_copy(g, k):
        i = g * SPLIT + k
        return pltpu.make_async_copy(own_piece(g, k), tile(held, jnp.int32(i), core), own_local.at[i])

    def inject(i, src):
        dst = tile(held, i, core)
        m = i * 2 + core
        start(src, dst, z_inject.at[i], z_recv.at[m], at_z(1, 0))
        start(src, dst, z_inject.at[UNITS + i], z_recv.at[m], at_z(-1, 1))
        start(src, dst, own_send.at[i], own_recv.at[i], sibling)

    def passes(c):
        return (w > 0) & ((w < 3) | (c == core))

    def ring(m):
        i, c = div(m, 2), rem(m, 2)
        at = tile(passed, i, c)

        @pl.when((w > 0) | (c == core))
        def _():
            wait_recv(at, z_recv.at[m])

            @pl.when(passes(c))
            def _():
                start(at, at, z_forward.at[m], z_recv.at[m], next_z)

            start(at, at, cross_send.at[m], cross_recv.at[m], sibling)

    def strip_rows(d, j):
        return pl.ds(pl.multiple_of(d * half + j * strip, strip), strip)

    def stream(d, j):
        at = strip_rows(d, j)
        n = d * STREAM + j
        wait_recv(other.at[at, :], y_recv.at[n])

        @pl.when(yl != 3 * (1 - d))
        def _():
            start(other.at[at, :], other.at[at, :], y_send.at[n], y_recv.at[n], at_y(1 - 2 * d))

    @pl.when(is_source)
    def _():
        for g in range(GROUPS):
            for k in range(SPLIT):
                inject(jnp.int32(g * SPLIT + k), own_piece(g, k))
        for g in range(GROUPS):
            for k in range(SPLIT):
                own_copy(g, k).start()

    @pl.when(w > 0)
    def _():
        to = rem(z, 4)
        e = gray(rem(x + 4 - to, 4))
        for g in range(GROUPS):
            for k in range(SPLIT):
                dst = bt.at[held, g, x, pl.ds(pl.multiple_of(core * rows + k * unit, unit), unit), :]
                arrival = x_recv.at[(rem(e, 3) + 2 + 3 * g) * SPLIT + k]
                start(own_piece(g, k), dst, x_send.at[g * SPLIT + k], arrival, (row, yh * 4 + to, yl))

    for d in range(2):

        @pl.when(yl == 3 * (1 - d))
        def _():
            for j in range(STREAM):
                at = strip_rows(d, j)
                n = d * STREAM + j
                start(a_ref.at[at, :], other.at[at, :], y_send.at[n], y_recv.at[n], at_y(1 - 2 * d))

    def tick(t):
        m = t - 4 * away

        @pl.when((m >= 0) & (m < 2 * UNITS))
        def _():
            ring(m)

        for d in range(2):
            j = t - HOP * (yl + 1 if d == 0 else 4 - yl)

            @pl.when((j >= 0) & (j < STREAM))
            def _():
                stream(d, j)

        i = t - 3

        @pl.when(is_source & (i >= 2 * SPLIT) & (i < UNITS))
        def _():
            src = tile(held, i, core)
            wait_recv(src, x_recv.at[i])
            inject(i, src)

    sib_w = rem(4 - w, 4)
    sib_away = sib_w + 4 * (1 - lax.min(sib_w, jnp.int32(1)))
    sib_passed = rel_half(rem(z + 8 + (1 - 2 * core) * sib_away, 8), yh)

    def arrived(g, b):
        first, after = [n * SPLIT for n in ((0, 3), (3, 5), (5, 6), (6, 8))[2 * g + b]]

        @pl.loop(2 * first, 2 * after)
        def _(m):
            i, c = div(m, 2), rem(m, 2)

            @pl.when((w > 0) | (c != core))
            def _():
                wait_recv(tile(sib_passed, i, c), cross_recv.at[m])

        @pl.when(is_source)
        def _():
            if g == 0 and b == 0:
                for i in range(2 * SPLIT):
                    own_copy(i // SPLIT, i % SPLIT).wait()

            @pl.loop(first, after)
            def _(i):
                wait_recv(tile(held, i, 1 - core), own_recv.at[i])

    def finish_operands():
        @pl.when(w > 0)
        def _():
            for i in range(2 * SPLIT):
                wait_send(bt.at[held, 0, x, pl.ds(0, unit), :], x_send.at[i])

        @pl.when(is_source)
        def _():
            @pl.loop(0, UNITS)
            def _(i):
                src = tile(held, i, core)
                wait_send(src, z_inject.at[i])
                wait_send(src, z_inject.at[UNITS + i])
                wait_send(src, own_send.at[i])

        @pl.loop(0, 2 * UNITS)
        def _(m):
            i, c = div(m, 2), rem(m, 2)
            at = tile(passed, i, c)

            @pl.when((w > 0) | (c == core))
            def _():
                wait_send(at, cross_send.at[m])

                @pl.when(passes(c))
                def _():
                    wait_send(at, z_forward.at[m])

        @pl.loop(0, 2 * STREAM)
        def _(n):
            at = pl.ds(pl.multiple_of(n * strip, strip), strip)
            wait_send(other.at[at, :], y_send.at[n])

    ahead, behind, across = rem(x + 1, 4), rem(x + 3, 4), rem(x + 2, 4)
    sent = []

    def send(src, dst, send_sem, recv_sem, device):
        copy = remote(src, dst, send_sem, recv_sem, device)
        copy.start()
        sent.append(copy.wait_send)

    class Sum:
        def __init__(self, part, relay, raw, summed, sends, recvs, chunk):
            self.part, self.relay, self.raw, self.summed = part, relay, raw, summed
            self.sends, self.recvs, self.mid = sends, recvs, chunk // 2
            self.slots = relay.shape[1]

        def at(self, piece, i, which):
            g, r = i
            rows_at = pl.ds((2 * r + which) * self.mid, self.mid)
            return (g, piece, rows_at, slice(None)) if g is not None else (piece, rows_at, slice(None))

        def slot(self, i):
            return i[0] * SQUARE + i[1] if i[0] is not None else i[1]

        def sems(self, kind, d, i):
            n = (kind * 2 + d) * self.slots + self.slot(i)
            return self.sends.at[n], self.recvs.at[n]

        def spread_far(self, i):
            n = self.slot(i)
            for d in range(2):
                src = self.part.at[self.at(across, i, d)]
                send(src, self.relay.at[d, n], *self.sems(0, d, i), at_x(1 - 2 * d))

        def spread_near(self, i):
            n = self.slot(i)
            for d in range(2):
                src = self.part.at[self.at(ahead if d == 0 else behind, i, 1 - d)]
                send(src, self.raw.at[d, n], *self.sems(1, d, i), at_x(1 - 2 * d))

        def pass_on(self, i):
            n = self.slot(i)
            for d in range(2):
                wait_recv(self.relay.at[d, n], self.sems(0, d, i)[1])
                at = self.at(ahead if d == 0 else behind, i, d)
                self.part[at] = self.part[at] + self.relay[d, n]
                send(self.part.at[at], self.summed.at[d, n], *self.sems(2, d, i), at_x(1 - 2 * d))

        def collect(self, i):
            n = self.slot(i)
            totals = []
            for d in range(2):
                wait_recv(self.raw.at[1 - d, n], self.sems(1, 1 - d, i)[1])
                wait_recv(self.summed.at[d, n], self.sems(2, d, i)[1])
                totals.append(self.part[self.at(x, i, d)] + self.raw[1 - d, n] + self.summed[d, n])
            return totals

    square_chunk, cube_chunk = rows // SQUARE, rows // CUBE
    square_sum = Sum(part1, relay1, raw1, summed1, rs1_send, rs1_recv, square_chunk)
    cube_sum = Sum(part2, relay2, raw2, summed2, rs2_send, rs2_recv, cube_chunk)

    def multiply_square(g, r, b):
        at = pl.ds(r * square_chunk, square_chunk)
        left = jnp.concatenate([a_ref[at, :], other[at, :]], axis=1)
        p, q = rem(x + b, 4), rem(x + b + 2, 4)
        right = jnp.concatenate([jnp.concatenate([bt[h, g, p], bt[h, g, q]], axis=1) for h in range(2)], axis=0)
        product = jnp.dot(left, right, preferred_element_type=F32)
        part1[g, p, at, :] = product[:, :cols]
        part1[g, q, at, :] = product[:, cols:]

    def round_square(g, r):
        mid = square_chunk // 2
        for d, total in enumerate(square_sum.collect((g, r))):
            sb[g, yl, pl.ds((2 * r + d) * mid, mid), :] = total.astype(BF16)

    def slot_of(y_from, y_at):
        return rem(div(y_from, 4) + div(y_at, 4), 2) * 4 + rem(y_from, 4)

    def gather(g, r, s):
        mid = square_chunk // 2
        slots = GROUPS * SQUARE
        n = g * SQUARE + r

        def part(d, last):
            return pl.ds((2 * r + d) * mid, mid) if last else pl.ds(r * square_chunk, square_chunk)

        for d in range(2):
            sign = 1 - 2 * d
            y_from = rem(y + 8 - sign * s, 8)
            if s > 0:
                here = sb.at[g, slot_of(y_from, y), part(d, s == 4), :]
                wait_recv(here, ag_recv.at[(d * 5 + s) * slots + n])
            if s < 4:
                at = part(d, s == 3)
                y_to = rem(y + 8 + sign, 8)
                send(
                    sb.at[g, slot_of(y_from, y), at, :],
                    sb.at[g, slot_of(y_from, y_to), at, :],
                    ag_send.at[(d * 5 + s) * slots + n],
                    ag_recv.at[(d * 5 + s + 1) * slots + n],
                    at_y(sign),
                )

    def multiply_cube(r):
        at = pl.ds(r * cube_chunk, cube_chunk)
        left = jnp.concatenate([sb[g, s, at, :] for s in range(8) for g in range(GROUPS)], axis=1)

        @pl.loop(0, 4)
        def _(p):
            right = jnp.concatenate(
                [jnp.concatenate([bt[h, g, p] for g in range(GROUPS)], axis=1) for h in range(2)], axis=0
            )
            part2[p, at, :] = jnp.dot(left, right, preferred_element_type=F32)

    def purify(r):
        mid = cube_chunk // 2
        for d, total in enumerate(cube_sum.collect((None, r))):
            at = pl.ds((2 * r + d) * mid, mid)
            own = jnp.concatenate([sb[g, yl, at, :] for g in range(GROUPS)], axis=1).astype(F32)
            out_ref[at, :] = 3.0 * own - 2.0 * total

    events, square_sends = [], []
    last = {}
    for g in range(GROUPS):
        begin, whole = [TICK * (2 * SPLIT * n + 4 * HOP) for n in ((3, 5), (6, 8))[g]]
        events += [(begin, lambda g=g: arrived(g, 0)), (whole, lambda g=g: arrived(g, 1))]
        for r in range(SQUARE):
            t = max(begin, ROWS[r * 4 // SQUARE] if g == 0 else 0) + r * DOT
            events.append((t, lambda g=g, r=r: (multiply_square(g, r, 0), square_sum.spread_far((g, r)))))
            t = whole + r * PERIOD
            events += [
                (t, lambda g=g, r=r: multiply_square(g, r, 1)),
                (t + PASS[g], lambda g=g, r=r: square_sum.pass_on((g, r))),
                (t + PASS[g], lambda g=g, r=r: square_sum.spread_near((g, r))),
                (t + COLLECT[g], lambda g=g, r=r: (round_square(g, r), gather(g, r, 0))),
            ]
            for s in range(1, 5):
                events.append((t + COLLECT[g] + RING * s, lambda g=g, r=r, s=s: gather(g, r, s)))
            last[r] = t + COLLECT[g] + RING * 4
    t = 0.0
    for r in range(CUBE):
        t = max(t + PERIOD, last[((r + 1) * SQUARE - 1) // CUBE])
        if r == 0:
            first = t
            events.append((first + QUIET, lambda: finish_operands()))
            events.append((first - 0.01, lambda: (square_sends.extend(sent), sent.clear())))
            events.append((first + QUIET, lambda: [wait() for wait in square_sends]))
        events += [
            (t, lambda r=r: (multiply_cube(r), cube_sum.spread_far((None, r)))),
            (t + PASS_CUBE, lambda r=r: cube_sum.pass_on((None, r))),
            (t if r == 0 else first + NEAR_CUBE + r * PERIOD_CUBE, lambda r=r: cube_sum.spread_near((None, r))),
            (first + COLLECT_CUBE + r * PERIOD_CUBE, lambda r=r: purify(r)),
        ]
    done = 0
    for t, event in sorted(events, key=lambda e: e[0]):
        due = min(TICKS, int(t / TICK))
        if due > done:
            pl.loop(done, due)(tick)
            done = due
        event()
    for wait in sent:
        wait()


def on_device(density):
    rows, width = density.shape
    share = width // 4
    cols = share // GROUPS
    dma = pltpu.SemaphoreType.DMA
    square_parts = pltpu.VMEM((2, GROUPS * SQUARE, rows // SQUARE // 2, cols), F32)
    cube_parts = pltpu.VMEM((2, CUBE, rows // CUBE // 2, share), F32)
    return pl.pallas_call(
        kernel,
        out_shape=jax.ShapeDtypeStruct((rows, share), F32),
        in_specs=[pl.BlockSpec(memory_space=pl.ANY)],
        out_specs=pl.BlockSpec(memory_space=pltpu.VMEM),
        scratch_shapes=[
            pltpu.VMEM((rows, width), BF16),
            pltpu.VMEM((GROUPS, rows, cols), BF16),
            pltpu.VMEM((rows, width), BF16),
            pltpu.VMEM((2, GROUPS, 4, 2 * rows, cols), BF16),
            pltpu.VMEM((GROUPS, 8, rows, cols), BF16),
            pltpu.VMEM((GROUPS, 4, rows, cols), F32),
            pltpu.VMEM((4, rows, share), F32),
            square_parts,
            square_parts,
            square_parts,
            cube_parts,
            cube_parts,
            cube_parts,
            dma((2 * SPLIT,)),
            dma((UNITS,)),
            dma((2 * STREAM,)),
            dma((2 * STREAM,)),
            dma((2 * UNITS,)),
            dma((2 * UNITS,)),
            dma((2 * UNITS,)),
            dma((2 * UNITS,)),
            dma((2 * UNITS,)),
            dma((UNITS,)),
            dma((UNITS,)),
            dma((2 * SPLIT,)),
            dma((GROUPS + 1,)),
            dma((6 * GROUPS * SQUARE,)),
            dma((6 * GROUPS * SQUARE,)),
            dma((6 * CUBE,)),
            dma((6 * CUBE,)),
            dma((10 * GROUPS * SQUARE,)),
            dma((10 * GROUPS * SQUARE,)),
        ],
        compiler_params=pltpu.CompilerParams(
            collective_id=0, has_side_effects=True, vmem_limit_bytes=48 * 1024 * 1024
        ),
    )(density)


def solution(mesh):
    return jax.shard_map(
        on_device, mesh=mesh, in_specs=(P("row", "col"),), out_specs=P("row", ("col", "depth")), check_vma=False
    )
```
